32 devices in a mesh: groups: 2 (over y), rows: 4 (over z), samples: 4 (over x, core).
Axes of the slice: x: 2, y: 2, z: 4, core: 2. Of those that a mesh axis runs over, the one named last changes fastest.
Arguments:
- ancestor: float32 [4096, 512], P(('groups', 'rows'), 'samples'), parts along dimension 0, may hold values from -6 to 6
- panels: float32 [2, 2, 1024, 256], P(None, None, 'rows', 'samples'), may hold values from -0.1875 to 0.1875
- row_map: int32 [2, 1024], P(None, 'rows'), may hold values from 0 to 511
- offsets: int32 [2], replicated, may hold values from 0 to 1536
- noise: float32 [4096, 512], P('groups', 'samples'), parts along dimension 0, may hold values from -6 to 6
- inverse: float32 [2, 2, 256, 256], P(None, None, 'rows'), as said below
- inner_link: float32 [2, 256, 256], P(None, 'rows'), may hold values from -0.375 to 0.375
- cross_link: float32 [2, 2, 256, 256], P(None, None, 'rows'), may hold values from -0.25 to 0.25
Outputs:
- solved: float32 [2, 2, 256, 1024], P(None, None, 'rows', ('groups', 'samples')), parts along dimension 3
The draws below stay inside these ranges and needn't reach their ends.
There are 2 independent parts, one for each index of `groups`. The reference program is written for one: setup_inputs(seed, part) draws one part's arguments, and reference() takes and returns one part's arrays. A program takes and returns all parts, laid end to end along the dimension named above; an argument that names none is the same for every part. Nothing has to cross between parts.
Inputs may be any that keep to these rules, and one draw needn't show every extreme that they name: inverse[p, b] is upper triangular: entry (i, j) is zero for j < i, and its diagonal is positive.
All inputs are finite; a program needn't handle non-finite values.
Results may differ from the reference program's by a relative error of at most 0.0003.
Values sent between devices are 32-bit elements; how exact they have to be, the bound alone decides.
A program may use at most 64 MiB of HBM per device.

```python
import math
import jax
import jax.numpy as jnp
from jax import lax

BLOCK = 256
ROW_DEV = 256
ANC_DEV = 512
NOISE = 2048
PANEL = 512
FRONT = 1024
ANC = 2048
SAMPLES = 512


def draw_inverse(key, part):
    diag_key, upper_key = jax.random.split(jax.random.fold_in(key, 7))
    diagonal = jax.random.uniform(diag_key, (2, 2, BLOCK), jnp.float32, 0.5, 1.5)
    upper = jax.random.normal(upper_key, (2, 2, BLOCK, BLOCK), jnp.float32) / math.sqrt(BLOCK)
    row_ids = jnp.arange(BLOCK)[:, None]
    col_ids = jnp.arange(BLOCK)[None, :]
    above = col_ids > row_ids
    on_diag = (col_ids == row_ids).astype(jnp.float32)
    return jnp.where(above, upper, 0.0) + diagonal[..., None] * on_diag


def place_ends(array, rng, low, top_value):
    extent = array.shape
    spot = [jax.random.randint(jax.random.fold_in(rng, axis), (), 0, extent[axis]) for axis in range(len(extent))]
    array = array.at[tuple(spot)].set(low)
    longest = extent.index(max(extent))
    spot[longest] = (spot[longest] + 1) % extent[longest]
    return array.at[tuple(spot)].set(top_value)


def shard_levels(stream_key, extent, pieces, smallest, high):
    level = 1.0
    for position, shards_of in pieces:
        steps = jax.random.uniform(jax.random.fold_in(jax.random.fold_in(stream_key, 6), position), (shards_of,), jnp.float32, smallest / len(pieces), high / len(pieces))
        level = level * jnp.repeat(jnp.exp(steps), extent[position] // shards_of).reshape((-1,) + (1,) * (len(extent) - 1 - position))
    return level


def gaussian(rng, dims, spread, limit, pieces=(), held_as=jnp.bfloat16):
    drawn = jax.random.normal(rng, dims, jnp.float32) * spread
    if len(pieces) > 0:
        drawn = shard_levels(rng, dims, pieces, -0.22, 0.18) * drawn
    return jnp.clip(drawn, min=-limit, max=limit).astype(held_as)


def setup_inputs(seed: int = 0, part: int = 0) -> dict:
    arg_keys = jax.random.split(jax.random.key(seed), 9)
    part_keys = jax.random.split(jax.random.fold_in(arg_keys[8], part), 9)
    return {
        "ancestor": gaussian(part_keys[0], (ANC, SAMPLES), 1.0, 6.0, ((0, 4), (1, 4)), jnp.float32),
        "panels": gaussian(arg_keys[1], (2, 2, FRONT, BLOCK), FRONT ** -0.5, 0.1875, ((2, 4), (3, 4)), jnp.float32),
        "row_map": place_ends(jax.random.randint(arg_keys[2], (2, FRONT), 0, ANC_DEV), jax.random.fold_in(arg_keys[2], 1), 0, ANC_DEV - 1).astype(jnp.int32),
        "offsets": jax.random.randint(arg_keys[3], (2,), 0, NOISE - PANEL + 1).astype(jnp.int32),
        "noise": gaussian(part_keys[4], (NOISE, SAMPLES), 1.0, 6.0, ((1, 4),), jnp.float32),
        "inverse": draw_inverse(jax.random.fold_in(arg_keys[8], 71), part),
        "inner_link": gaussian(arg_keys[6], (2, BLOCK, BLOCK), BLOCK ** -0.5, 0.375, ((1, 4),), jnp.float32),
        "cross_link": gaussian(arg_keys[7], (2, 2, BLOCK, BLOCK), (2 * BLOCK) ** -0.5, 0.25, ((2, 4),), jnp.float32),
    }


def product(left, right):
    return jnp.dot(left, right, precision=lax.Precision.HIGHEST, preferred_element_type=jnp.float32)


def reference(ancestor, panels, row_map, offsets, noise, inverse, inner_link, cross_link):
    owners = (jnp.arange(FRONT, dtype=jnp.int32) // ROW_DEV) * ANC_DEV
    solved = [[None, None], [None, None]]
    for which_panel in (1, 0):
        indices = (row_map[which_panel] + owners).astype(jnp.int32)
        front_rows = jnp.take(ancestor, indices, axis=0)
        window = lax.dynamic_slice_in_dim(noise, offsets[which_panel], 2 * BLOCK, 0)
        for which_block in (1, 0):
            partial_value = product(panels[which_panel, which_block].T, front_rows)
            if which_block == 0:
                partial_value = partial_value + product(inner_link[which_panel].T, solved[which_panel][1])
            if which_panel == 0:
                for earlier in (0, 1):
                    partial_value = partial_value + product(cross_link[which_block, earlier].T, solved[1][earlier])
            target = window[which_block * BLOCK:(which_block + 1) * BLOCK]
            solved[which_panel][which_block] = product(inverse[which_panel, which_block], target - partial_value)
    return jnp.stack([jnp.stack(solved[0]), jnp.stack(solved[1])])
```

```python
import functools

import jax
import jax.numpy as jnp
from jax import lax
from jax.experimental import pallas as pl
from jax.experimental.pallas import tpu as pltpu
from jax.sharding import PartitionSpec as P

F32 = jnp.float32
BF16 = jnp.bfloat16
NN = ((1,), (0,))
NT = ((1,), (1,))


def product(left, right):
    return jnp.dot(left, right, precision=lax.Precision.HIGHEST, preferred_element_type=F32)


def apply_inverse(target, partial_value, inverse_rows):
    rows_here = inverse_rows.shape[0]
    share = lax.psum_scatter(partial_value, "rows", scatter_dimension=0, tiled=True)
    first_own = lax.axis_index("rows") * rows_here
    residue = lax.dynamic_slice_in_dim(target, first_own, rows_here, 0) - share
    return product(inverse_rows, lax.all_gather(residue, "rows", axis=0, tiled=True))


def plain(ancestor, panels, row_map, offsets, noise, inverse, inner_link, cross_link):
    block_rows = inverse.shape[3]
    solved = [[None, None], [None, None]]
    for p in (1, 0):
        front_rows = jnp.take(ancestor, row_map[p], axis=0)
        window = lax.dynamic_slice_in_dim(noise, offsets[p], 2 * block_rows, 0)
        for b in (1, 0):
            whole = lax.all_gather(panels[p, b], "samples", axis=1, tiled=True)
            partial_value = product(whole.T, front_rows)
            if b == 0:
                partial_value = partial_value + product(inner_link[p].T, solved[p][1])
            if p == 0:
                for e in (0, 1):
                    partial_value = partial_value + product(cross_link[b, e].T, solved[1][e])
            target = window[b * block_rows : (b + 1) * block_rows]
            solved[p][b] = apply_inverse(target, partial_value, inverse[p, b])
    return jnp.stack([jnp.stack(solved[0]), jnp.stack(solved[1])])


def split(a):
    hi = a.astype(BF16)
    return hi, (a - hi.astype(F32)).astype(BF16)


def dot(a, b, dims):
    return lax.dot_general(a, b, (dims, ((), ())), preferred_element_type=F32)


def mm(a, b, dims):
    ah, al = split(a)
    bh, bl = split(b)
    m = a.shape[0]
    both = dot(jnp.concatenate([ah, al], 0), bh, dims)
    return both[:m] + (both[m:] + dot(ah, bl, dims))


def kernel(
    n, rm_h, off_h, anc_h, pan_h, noise_h, inv_h, lnk_h, crs_h, out,
    rm, off, anc, nz, mats, pk, fr, tt, y1, y0, r1, r0, osend, orecv,
    loc, pxs, pxr, pcs, pcr, prs, prr, zs, zr, ms, mr, cs, cr, as_, ar, bs, br, oss, osr,
):
    y = lax.axis_index("groups")
    z = lax.axis_index("rows")
    s = lax.axis_index("samples")
    x, c = s // 2, s % 2
    sx = (s + 2) % 4
    sib = s + 1 - 2 * c
    to_x, to_y, to_c = {"samples": sx}, {"groups": 1 - y}, {"samples": sib}
    to_d = {"groups": 1 - y, "samples": sx}
    block = mats.shape[3]
    share = mats.shape[2]
    piece = share // 8
    lanes = anc.shape[1]
    w = lanes // n

    barrier = pltpu.get_barrier_semaphore()
    peers = [{"rows": (z + k) % n} for k in range(1, n)] + [to_x, to_y, to_c, to_d]
    for peer in peers:
        pl.semaphore_signal(barrier, inc=1, device_id=peer, device_id_type=pl.DeviceIdType.MESH)

    local = [
        pltpu.make_async_copy(rm_h, rm, loc.at[0]),
        pltpu.make_async_copy(off_h, off, loc.at[1]),
        pltpu.make_async_copy(anc_h, anc, loc.at[2]),
        pltpu.make_async_copy(pan_h, pk.at[:, :, s], loc.at[3]),
        pltpu.make_async_copy(noise_h, nz, loc.at[4]),
        pltpu.make_async_copy(inv_h.at[0:2], mats.at[0:2, z], loc.at[5]),
        pltpu.make_async_copy(lnk_h.at[0:1], mats.at[2:3, z], loc.at[6]),
        pltpu.make_async_copy(inv_h.at[2:4], mats.at[3:5, z], loc.at[7]),
        pltpu.make_async_copy(lnk_h.at[1:2], mats.at[5:6, z], loc.at[8]),
        pltpu.make_async_copy(crs_h, mats.at[6:10, z], loc.at[9]),
    ]
    for copy in local:
        copy.start()

    pl.semaphore_wait(barrier, len(peers))

    pending = []

    def remote(src, dst, ss, rs, where):
        return pltpu.make_async_remote_copy(
            src_ref=src, dst_ref=dst, send_sem=ss, recv_sem=rs,
            device_id=where, device_id_type=pl.DeviceIdType.MESH,
        )

    def go(copy):
        copy.start()
        pending.append(copy)
        return copy

    def at_rows(q):
        return pl.ds(pl.multiple_of(q * piece, piece), piece)

    order = [(1, 1), (1, 0), (0, 1), (0, 0)]
    q = c * 4 + x * 2 + y
    groups = [(0, 3), (3, 6), (6, 10)]
    sources = [
        [(inv_h, 0, 2, 0), (lnk_h, 0, 1, 2)],
        [(inv_h, 2, 4, 3), (lnk_h, 1, 2, 5)],
        [(crs_h, 0, 4, 6)],
    ]
    stage_z = {}

    def send_z(g):
        for k in range(1, n):
            for h, (ref, lo, hi, at) in enumerate(sources[g]):
                stage_z[g, k, h] = go(remote(
                    ref.at[lo:hi, at_rows(q)], mats.at[at : at + hi - lo, z, at_rows(q)],
                    zs.at[g, k, h], zr.at[g, k, h], {"rows": (z + k) % n},
                ))

    pan_x, pan_c = {}, {}

    def send_p(p):
        for b in (1, 0):
            pan_x[p, b] = go(remote(pan_h.at[p, b], pk.at[p, b, s], pxs.at[p, b], pxr.at[p, b], to_x))
        pan_c[p] = go(remote(pan_h.at[p], pk.at[p, :, s], pcs.at[p], pcr.at[p], to_c))

    send_p(1)
    send_z(0)
    send_p(0)
    send_z(1)
    send_z(2)

    for i in range(3):
        local[i].wait()

    def gather(p):
        def rows8(i, carry):
            for r in range(8):
                fr[p, pl.ds(i * 8 + r, 1), :] = anc[pl.ds(rm[p, i * 8 + r], 1), :]
            return carry

        lax.fori_loop(0, fr.shape[1] // 8, rows8, 0)

    gather(1)
    ft = fr[1].T
    fth, ftl = split(ft)
    ftb = jnp.concatenate([fth, ftl], 0)

    pan_r = {}

    def relay_p(p, b):
        pan_x[p, b].wait_recv()
        pan_r[p, b] = go(remote(pk.at[p, b, sx], pk.at[p, b, sx], prs.at[p, b], prr.at[p, b], to_c))

    relay_p(1, 1)
    relay_p(1, 0)
    local[3].wait()
    pan_c[1].wait_recv()

    def sums_1(b):
        pan_r[1, b].wait_recv()
        ph, plo = split(pk[1, b].reshape(block, block))
        both = dot(ftb, ph, NT)
        y1[b] = both[:lanes] + (both[lanes:] + dot(fth, plo, NT))
        for k in range(1, n):
            zz = (z + k) % n
            go(remote(
                y1.at[b, pl.ds(pl.multiple_of(zz * w, w), w)], r1.at[k, b], as_.at[k, b], ar.at[k, b], {"rows": zz}
            ))

    sums_1(1)
    sums_1(0)

    stage_m = {}

    def spread(g):
        lo, hi = groups[g]
        for k in range(1, n):
            zz = (z + n - k) % n
            for h in range(len(sources[g])):
                stage_z[g, k, h].wait_recv()
            ref = mats.at[lo:hi, zz, at_rows(q)]
            for d, where in enumerate((to_x, to_y, to_d)):
                stage_m[g, k, d] = go(remote(ref, ref, ms.at[g, k, d], mr.at[g, k, d], where))

    spread(0)
    relay_p(0, 1)
    relay_p(0, 0)
    spread(1)
    gather(0)
    local[4].wait()
    spread(2)
    pan_c[0].wait_recv()
    rest = {}
    for b in (1, 0):
        pan_r[0, b].wait_recv()
        start = pl.ds(off[0] + b * block, block)
        rest[b] = nz[start, :] * (1.0 / n) - mm(pk[0, b].reshape(block, block), fr[0], NN)
    tt[...] = nz[pl.ds(off[1], 2 * block), :].T

    stage_c = {}

    def join(g):
        lo, hi = groups[g]
        for k in range(1, n):
            for d in range(3):
                stage_m[g, k, d].wait_recv()
            zz = (z + n - k) % n
            ref = mats.at[lo:hi, zz, pl.ds(pl.multiple_of(c * 4 * piece, 4 * piece), 4 * piece)]
            stage_c[g, k] = go(remote(ref, ref, cs.at[g, k], cr.at[g, k], to_c))

    def joined(g):
        for k in range(1, n):
            stage_c[g, k].wait_recv()

    def matrix(i):
        return mats[i].reshape(block, block)

    def sums_0(b, value):
        y0[b] = value
        for k in range(1, n):
            zz = (z + k) % n
            go(remote(
                y0.at[b, pl.ds(pl.multiple_of(zz * share, share), share)], r0.at[k, b], bs.at[k, b], br.at[k, b], {"rows": zz}
            ))

    join(0)
    for i in range(5, 10):
        local[i].wait()
    joined(0)
    part = mm(matrix(1), rest[1], NN)
    sums_0(1, part)
    sums_0(0, mm(matrix(0), rest[0] - mm(matrix(2).T, part, NN), NN))

    join(1)
    join(2)
    joined(1)

    def residue(b):
        total = y1[b, pl.ds(pl.multiple_of(z * w, w), w), :]
        for k in range(1, n):
            zz = (z + k) % n
            remote(
                y1.at[b, pl.ds(pl.multiple_of(zz * w, w), w)], r1.at[k, b], as_.at[k, b], ar.at[k, b], {"rows": zz}
            ).wait_recv()
            total = total + r1[k, b]
        return tt[pl.ds(pl.multiple_of(z * w, w), w), b * block : (b + 1) * block] - total

    def back(p, first, second):
        for i in range(n):
            cut = slice(i * share, (i + 1) * share)
            osend[p, i] = jnp.concatenate([first[:, cut], second[:, cut]], axis=1)
        orecv[p, z] = osend[p, z]
        for k in range(1, n):
            go(remote(osend.at[p, (z + k) % n], orecv.at[p, z], oss.at[k, p], osr.at[k, p], {"rows": (z + k) % n}))

    s11 = mm(residue(1), matrix(4), NT)
    s10 = mm(residue(0) - mm(s11, matrix(5), NN), matrix(3), NT)
    back(1, s10, s11)
    joined(2)
    v01 = mm(-(mm(s10, matrix(8), NN) + mm(s11, matrix(9), NN)), matrix(1), NT)
    v00 = mm(-(mm(s10, matrix(6), NN) + mm(s11, matrix(7), NN) + mm(v01, matrix(2), NN)), matrix(0), NT)
    back(0, v00, v01)

    def landed(p):
        for k in range(1, n):
            src = (z + n - k) % n
            remote(osend.at[p, src], orecv.at[p, src], oss.at[k, p], osr.at[k, p], {"rows": src}).wait_recv()
        return orecv[p].reshape(lanes, 2 * share).T.reshape(2, share, lanes)

    out[1] = landed(1)
    total = []
    for b in (0, 1):
        own = y0[b, pl.ds(pl.multiple_of(z * share, share), share), :]
        for k in range(1, n):
            zz = (z + k) % n
            remote(
                y0.at[b, pl.ds(pl.multiple_of(zz * share, share), share)], r0.at[k, b], bs.at[k, b], br.at[k, b], {"rows": zz}
            ).wait_recv()
            own = own + r0[k, b]
        total.append(own)
    last = landed(0)
    for b in (0, 1):
        out[0, b] = last[b] + total[b]

    for copy in pending:
        copy.wait_send()


def fused(n, ancestor, panels, row_map, offsets, noise, inverse, inner_link, cross_link):
    share, block = inverse.shape[2:]
    lanes = ancestor.shape[1]
    w = lanes // n
    cols, rows = panels.shape[3], panels.shape[2]
    dma = pltpu.SemaphoreType.DMA
    hbm = pl.BlockSpec(memory_space=pltpu.HBM)
    return pl.pallas_call(
        functools.partial(kernel, n),
        name="substitute",
        out_shape=jax.ShapeDtypeStruct((2, 2, share, lanes), F32),
        in_specs=[hbm] * 8,
        out_specs=pl.BlockSpec(memory_space=pltpu.VMEM),
        scratch_shapes=[
            pltpu.SMEM(row_map.shape, jnp.int32),
            pltpu.SMEM(offsets.shape, jnp.int32),
            pltpu.VMEM(ancestor.shape, F32),
            pltpu.VMEM(noise.shape, F32),
            pltpu.VMEM((10, n, share, block), F32),
            pltpu.VMEM((2, 2, 4, cols, rows), F32),
            pltpu.VMEM((2, rows, lanes), F32),
            pltpu.VMEM((lanes, 2 * block), F32),
            pltpu.VMEM((2, lanes, block), F32),
            pltpu.VMEM((2, block, lanes), F32),
            pltpu.VMEM((n, 2, w, block), F32),
            pltpu.VMEM((n, 2, share, lanes), F32),
            pltpu.VMEM((2, n, w, 2 * share), F32),
            pltpu.VMEM((2, n, w, 2 * share), F32),
            dma((10,)),
            dma((2, 2)), dma((2, 2)),
            dma((2,)), dma((2,)),
            dma((2, 2)), dma((2, 2)),
            dma((3, n, 2)), dma((3, n, 2)),
            dma((3, n, 3)), dma((3, n, 3)),
            dma((3, n)), dma((3, n)),
            dma((n, 2)), dma((n, 2)),
            dma((n, 2)), dma((n, 2)),
            dma((n, 2)), dma((n, 2)),
        ],
        compiler_params=pltpu.CompilerParams(
            collective_id=0, has_side_effects=True, vmem_limit_bytes=62 * 1024 * 1024
        ),
    )(
        row_map, offsets, ancestor, jnp.swapaxes(panels, 2, 3), noise,
        inverse.reshape(4, share, block), inner_link, cross_link.reshape(4, share, block),
    )


def solution(mesh):
    placed = (
        P(("groups", "rows"), "samples"),
        P(None, None, "rows", "samples"),
        P(None, "rows"),
        P(),
        P("groups", "samples"),
        P(None, None, "rows", None),
        P(None, "rows", None),
        P(None, None, "rows", None),
    )
    n = mesh.shape["rows"]

    def local(ancestor, panels, row_map, offsets, noise, inverse, inner_link, cross_link):
        args = (ancestor, panels, row_map, offsets, noise, inverse, inner_link, cross_link)
        fits = (
            mesh.shape["groups"] == 2
            and mesh.shape["samples"] == 4
            and n == 4
            and ancestor.shape[1] == 128
            and inverse.shape[2] % 64 == 0
            and row_map.shape[1] % 128 == 0
        )
        return fused(n, *args) if fits else plain(*args)

    return jax.shard_map(
        local,
        mesh=mesh,
        in_specs=placed,
        out_specs=P(None, None, "rows", ("groups", "samples")),
        check_vma=False,
    )
```

```python
import functools

import jax
import jax.numpy as jnp
from jax import lax
from jax.experimental import pallas as pl
from jax.experimental.pallas import tpu as pltpu
from jax.sharding import PartitionSpec as P

F32 = jnp.float32
BF16 = jnp.bfloat16
NN = ((1,), (0,))
NT = ((1,), (1,))


def product(left, right):
    return jnp.dot(left, right, precision=lax.Precision.HIGHEST, preferred_element_type=F32)


def apply_inverse(target, partial_value, inverse_rows):
    rows_here = inverse_rows.shape[0]
    share = lax.psum_scatter(partial_value, "rows", scatter_dimension=0, tiled=True)
    first_own = lax.axis_index("rows") * rows_here
    residue = lax.dynamic_slice_in_dim(target, first_own, rows_here, 0) - share
    return product(inverse_rows, lax.all_gather(residue, "rows", axis=0, tiled=True))


def plain(ancestor, panels, row_map, offsets, noise, inverse, inner_link, cross_link):
    block_rows = inverse.shape[3]
    solved = [[None, None], [None, None]]
    for p in (1, 0):
        front_rows = jnp.take(ancestor, row_map[p], axis=0)
        window = lax.dynamic_slice_in_dim(noise, offsets[p], 2 * block_rows, 0)
        for b in (1, 0):
            whole = lax.all_gather(panels[p, b], "samples", axis=1, tiled=True)
            partial_value = product(whole.T, front_rows)
            if b == 0:
                partial_value = partial_value + product(inner_link[p].T, solved[p][1])
            if p == 0:
                for e in (0, 1):
                    partial_value = partial_value + product(cross_link[b, e].T, solved[1][e])
            target = window[b * block_rows : (b + 1) * block_rows]
            solved[p][b] = apply_inverse(target, partial_value, inverse[p, b])
    return jnp.stack([jnp.stack(solved[0]), jnp.stack(solved[1])])


def split(a):
    hi = a.astype(BF16)
    return hi, (a - hi.astype(F32)).astype(BF16)


def dot(a, b, dims):
    return lax.dot_general(a, b, (dims, ((), ())), preferred_element_type=F32)


def mm(a, b, dims):
    ah, al = split(a)
    bh, bl = split(b)
    m = a.shape[0]
    both = dot(jnp.concatenate([ah, al], 0), bh, dims)
    return both[:m] + (both[m:] + dot(ah, bl, dims))


def kernel(
    n, rm_h, off_h, anc_h, pan_h, noise_h, inv_h, lnk_h, crs_h, out,
    rm, off, anc, nz, mats, pk, fr, tt, y1, y0, r1, r0, osend, orecv,
    loc, sent, pxr, pcr, prr, zr, mr, cr, ar, br, osr,
):
    y = lax.axis_index("groups")
    z = lax.axis_index("rows")
    s = lax.axis_index("samples")
    x, c = s // 2, s % 2
    sx = (s + 2) % 4
    sib = s + 1 - 2 * c
    to_x, to_y, to_c = {"samples": sx}, {"groups": 1 - y}, {"samples": sib}
    to_d = {"groups": 1 - y, "samples": sx}
    block = mats.shape[3]
    share = mats.shape[2]
    piece = share // 8
    lanes = anc.shape[1]
    w = lanes // n

    barrier = pltpu.get_barrier_semaphore()
    peers = [{"rows": (z + k) % n} for k in range(1, n)] + [to_d, to_x, to_y, to_c]
    for peer in peers:
        pl.semaphore_signal(barrier, inc=1, device_id=peer, device_id_type=pl.DeviceIdType.MESH)

    local = [
        pltpu.make_async_copy(rm_h, rm, loc.at[0]),
        pltpu.make_async_copy(anc_h, anc, loc.at[1]),
        pltpu.make_async_copy(pan_h, pk.at[:, :, s], loc.at[2]),
        pltpu.make_async_copy(off_h, off, loc.at[3]),
        pltpu.make_async_copy(inv_h.at[0:2], mats.at[0:2, z], loc.at[5]),
        pltpu.make_async_copy(lnk_h.at[0:1], mats.at[2:3, z], loc.at[5]),
        pltpu.make_async_copy(inv_h.at[2:4], mats.at[3:5, z], loc.at[5]),
        pltpu.make_async_copy(lnk_h.at[1:2], mats.at[5:6, z], loc.at[5]),
        pltpu.make_async_copy(crs_h, mats.at[6:10, z], loc.at[5]),
        pltpu.make_async_copy(noise_h, nz, loc.at[4]),
    ]
    for copy in local[:2]:
        copy.start()

    def remote(src, dst, ss, rs, where):
        return pltpu.make_async_remote_copy(
            src_ref=src, dst_ref=dst, send_sem=ss, recv_sem=rs,
            device_id=where, device_id_type=pl.DeviceIdType.MESH,
        )

    def go(src, dst, ss, rs, where):
        remote(src, dst, sent.at[ss], rs, where).start()

    def whole(ref, sem):
        pltpu.make_async_copy(ref, ref, sem).wait()

    def rows_at(index, size):
        return pl.ds(pl.multiple_of(index * size, size), size)

    q = c * 4 + x * 2 + y
    groups = [(0, 3), (3, 6), (6, 10)]
    sources = [
        [(inv_h, 0, 2, 0), (lnk_h, 0, 1, 2)],
        [(inv_h, 2, 4, 3), (lnk_h, 1, 2, 5)],
        [(crs_h, 0, 4, 6)],
    ]

    def send_z(g):
        for k in range(1, n):
            for ref, lo, hi, at in sources[g]:
                go(
                    ref.at[lo:hi, rows_at(q, piece)], mats.at[at : at + hi - lo, z, rows_at(q, piece)],
                    1, zr.at[g, k], {"rows": (z + k) % n},
                )

    def send_p(p):
        for b in (1, 0):
            go(pan_h.at[p, b], pk.at[p, b, s], 0, pxr.at[p, b], to_x)
        go(pan_h.at[p], pk.at[p, :, s], 0, pcr.at[p], to_c)

    def relay_p(p, b):
        whole(pk.at[p, b, sx], pxr.at[p, b])
        go(pk.at[p, b, sx], pk.at[p, b, sx], 0, prr.at[p, b], to_c)

    def sibling_p(p):
        whole(pk.at[p, :, sib], pcr.at[p])

    def relayed_p(p, b):
        whole(pk.at[p, b, sib], prr.at[p, b])

    def gather(p):
        def rows8(i, carry):
            for r in range(8):
                fr[p, pl.ds(i * 8 + r, 1), :] = anc[pl.ds(rm[p, i * 8 + r], 1), :]
            return carry

        lax.fori_loop(0, fr.shape[1] // 8, rows8, 0)

    def spread(g):
        lo, hi = groups[g]
        for k in range(1, n):
            zz = (z + n - k) % n
            ref = mats.at[lo:hi, zz, rows_at(q, piece)]
            whole(ref, zr.at[g, k])
            for where in (to_d, to_x, to_y):
                go(ref, ref, 1, mr.at[g, k], where)

    def join(g):
        lo, hi = groups[g]
        for k in range(1, n):
            zz = (z + n - k) % n
            whole(mats.at[lo:hi, zz, 0 : 3 * piece], mr.at[g, k])
            ref = mats.at[lo:hi, zz, rows_at(c, 4 * piece)]
            go(ref, ref, 1, cr.at[g], to_c)

    def joined(g):
        lo, hi = groups[g]
        whole(mats.at[lo:hi, 0 : n - 1, 0 : 4 * piece], cr.at[g])

    def matrix(i):
        return mats[i].reshape(block, block)

    def sums_1(b, fh, fb):
        ph, low = split(pk[1, b].reshape(block, block))
        both = dot(fb, ph, NT)
        y1[b] = both[:lanes] + (both[lanes:] + dot(fh, low, NT))
        for k in range(1, n):
            zz = (z + k) % n
            go(y1.at[b, rows_at(zz, w)], r1.at[k, b], 2, ar.at[b], {"rows": zz})

    def sums_0(b, value):
        y0[b] = value
        for k in range(1, n):
            zz = (z + k) % n
            go(y0.at[b, rows_at(zz, share)], r0.at[k, b], 3, br.at[b], {"rows": zz})

    def residue(b):
        whole(r1.at[1:n, b], ar.at[b])
        total = y1[b, rows_at(z, w), :]
        for k in range(1, n):
            total = total + r1[k, b]
        return tt[rows_at(z, w), b * block : (b + 1) * block] - total

    def back(p, first, second):
        for i in range(n):
            cut = slice(i * share, (i + 1) * share)
            osend[p, i] = jnp.concatenate([first[:, cut], second[:, cut]], axis=1)
        orecv[p, z] = osend[p, z]
        for k in range(1, n):
            zz = (z + k) % n
            go(osend.at[p, zz], orecv.at[p, z], 4, osr.at[p], {"rows": zz})

    def landed(p):
        whole(orecv.at[p, 0 : n - 1], osr.at[p])
        return orecv[p].reshape(lanes, 2 * share).T.reshape(2, share, lanes)

    pl.semaphore_wait(barrier, len(peers))
    send_p(1)
    send_z(0)
    local[2].start()
    send_p(0)
    send_z(1)
    send_z(2)
    for copy in local[3:]:
        copy.start()

    local[0].wait()
    local[1].wait()
    gather(1)
    fh, low = split(fr[1].T)
    fb = jnp.concatenate([fh, low], 0)
    relay_p(1, 1)
    relay_p(1, 0)
    spread(0)
    local[2].wait()
    sibling_p(1)
    relayed_p(1, 1)
    sums_1(1, fh, fb)
    relayed_p(1, 0)
    sums_1(0, fh, fb)
    gather(0)
    relay_p(0, 1)
    relay_p(0, 0)
    spread(1)
    local[3].wait()
    whole(mats.at[:, z], loc.at[5])
    local[9].wait()
    sibling_p(0)
    rest = {}
    for b in (1, 0):
        relayed_p(0, b)
        rest[b] = nz[pl.ds(off[0] + b * block, block), :] * (1.0 / n) - mm(pk[0, b].reshape(block, block), fr[0], NN)
    spread(2)
    tt[...] = nz[pl.ds(off[1], 2 * block), :].T
    join(0)
    joined(0)
    part = mm(matrix(1), rest[1], NN)
    sums_0(1, part)
    sums_0(0, mm(matrix(0), rest[0] - mm(matrix(2).T, part, NN), NN))
    join(1)
    joined(1)
    s11 = mm(residue(1), matrix(4), NT)
    s10 = mm(residue(0) - mm(s11, matrix(5), NN), matrix(3), NT)
    back(1, s10, s11)
    join(2)
    joined(2)
    s1 = jnp.concatenate([s10, s11], axis=1)
    v01 = mm(-mm(s1, mats[8:10].reshape(2 * block, block), NN), matrix(1), NT)
    v00 = mm(-(mm(s1, mats[6:8].reshape(2 * block, block), NN) + mm(v01, matrix(2), NN)), matrix(0), NT)
    back(0, v00, v01)
    out[1] = landed(1)
    total = []
    for b in (0, 1):
        whole(r0.at[1:n, b], br.at[b])
        own = y0[b, rows_at(z, share), :]
        for k in range(1, n):
            own = own + r0[k, b]
        total.append(own)
    last = landed(0)
    for b in (0, 1):
        out[0, b] = last[b] + total[b]
    whole(pk.at[:, :, 0:3], sent.at[0])
    whole(mats.at[:, 0 : n - 1], sent.at[1])
    whole(r1.at[1:n], sent.at[2])
    whole(r0.at[1:n], sent.at[3])
    whole(orecv.at[:, 0 : n - 1], sent.at[4])


def fused(n, ancestor, panels, row_map, offsets, noise, inverse, inner_link, cross_link):
    share, block = inverse.shape[2:]
    lanes = ancestor.shape[1]
    w = lanes // n
    cols, rows = panels.shape[3], panels.shape[2]
    dma = pltpu.SemaphoreType.DMA
    hbm = pl.BlockSpec(memory_space=pltpu.HBM)
    args = (
        row_map, offsets, ancestor, jnp.swapaxes(panels, 2, 3), noise,
        inverse.reshape(4, share, block), inner_link, cross_link.reshape(4, share, block),
    )
    return pl.pallas_call(
        functools.partial(kernel, n),
        name="substitute",
        out_shape=jax.ShapeDtypeStruct((2, 2, share, lanes), F32),
        in_specs=[hbm] * 8,
        out_specs=pl.BlockSpec(memory_space=pltpu.VMEM),
        scratch_shapes=[
            pltpu.SMEM(row_map.shape, jnp.int32),
            pltpu.SMEM(offsets.shape, jnp.int32),
            pltpu.VMEM(ancestor.shape, F32),
            pltpu.VMEM(noise.shape, F32),
            pltpu.VMEM((10, n, share, block), F32),
            pltpu.VMEM((2, 2, 4, cols, rows), F32),
            pltpu.VMEM((2, rows, lanes), F32),
            pltpu.VMEM((lanes, 2 * block), F32),
            pltpu.VMEM((2, lanes, block), F32),
            pltpu.VMEM((2, block, lanes), F32),
            pltpu.VMEM((n, 2, w, block), F32),
            pltpu.VMEM((n, 2, share, lanes), F32),
            pltpu.VMEM((2, n, w, 2 * share), F32),
            pltpu.VMEM((2, n, w, 2 * share), F32),
            dma((6,)), dma((5,)),
            dma((2, 2)), dma((2,)), dma((2, 2)),
            dma((3, n)), dma((3, n)), dma((3,)),
            dma((2,)), dma((2,)), dma((2,)),
        ],
        compiler_params=pltpu.CompilerParams(
            collective_id=0, has_side_effects=True, vmem_limit_bytes=40 * 1024 * 1024
        ),
    )(*[pltpu.with_memory_space_constraint(a, pltpu.HBM) for a in args])


def solution(mesh):
    placed = (
        P(("groups", "rows"), "samples"),
        P(None, None, "rows", "samples"),
        P(None, "rows"),
        P(),
        P("groups", "samples"),
        P(None, None, "rows", None),
        P(None, "rows", None),
        P(None, None, "rows", None),
    )
    n = mesh.shape["rows"]

    def local(ancestor, panels, row_map, offsets, noise, inverse, inner_link, cross_link):
        args = (ancestor, panels, row_map, offsets, noise, inverse, inner_link, cross_link)
        fits = (
            mesh.shape["groups"] == 2
            and mesh.shape["samples"] == 4
            and n == 4
            and ancestor.shape[1] == 128
            and inverse.shape[2] % 64 == 0
            and row_map.shape[1] % 128 == 0
        )
        return fused(n, *args) if fits else plain(*args)

    return jax.shard_map(
        local,
        mesh=mesh,
        in_specs=placed,
        out_specs=P(None, None, "rows", ("groups", "samples")),
        check_vma=False,
    )
```

```python
import functools

import jax
import jax.numpy as jnp
from jax import lax
from jax.experimental import pallas as pl
from jax.experimental.pallas import tpu as pltpu
from jax.sharding import PartitionSpec as P

F32 = jnp.float32
BF16 = jnp.bfloat16
NN = ((1,), (0,))
NT = ((1,), (1,))


def product(left, right):
    return jnp.dot(left, right, precision=lax.Precision.HIGHEST, preferred_element_type=F32)


def apply_inverse(target, partial_value, inverse_rows):
    rows_here = inverse_rows.shape[0]
    share = lax.psum_scatter(partial_value, "rows", scatter_dimension=0, tiled=True)
    first_own = lax.axis_index("rows") * rows_here
    residue = lax.dynamic_slice_in_dim(target, first_own, rows_here, 0) - share
    return product(inverse_rows, lax.all_gather(residue, "rows", axis=0, tiled=True))


def plain(ancestor, panels, row_map, offsets, noise, inverse, inner_link, cross_link):
    block_rows = inverse.shape[3]
    solved = [[None, None], [None, None]]
    for p in (1, 0):
        front_rows = jnp.take(ancestor, row_map[p], axis=0)
        window = lax.dynamic_slice_in_dim(noise, offsets[p], 2 * block_rows, 0)
        for b in (1, 0):
            whole = lax.all_gather(panels[p, b], "samples", axis=1, tiled=True)
            partial_value = product(whole.T, front_rows)
            if b == 0:
                partial_value = partial_value + product(inner_link[p].T, solved[p][1])
            if p == 0:
                for e in (0, 1):
                    partial_value = partial_value + product(cross_link[b, e].T, solved[1][e])
            target = window[b * block_rows : (b + 1) * block_rows]
            solved[p][b] = apply_inverse(target, partial_value, inverse[p, b])
    return jnp.stack([jnp.stack(solved[0]), jnp.stack(solved[1])])


def split(a):
    hi = a.astype(BF16)
    return hi, (a - hi.astype(F32)).astype(BF16)


def dot(a, b, dims):
    return lax.dot_general(a, b, (dims, ((), ())), preferred_element_type=F32)


def mm(a, b, dims):
    ah, al = split(a)
    bh, bl = split(b)
    m = a.shape[0]
    both = dot(jnp.concatenate([ah, al], 0), bh, dims)
    return both[:m] + (both[m:] + dot(ah, bl, dims))


def kernel(
    n, rm_h, off_h, anc_h, pan_h, noise_h, inv_h, lnk_h, crs_h, out,
    rm, off, anc, nz, tm, cm, pk, fr, tt, y1, y0, r1, r0, osend, orecv,
    loc, sent, pxr, pcr, prr, zr, mr, cr, ar, br, osr,
):
    y = lax.axis_index("groups")
    z = lax.axis_index("rows")
    s = lax.axis_index("samples")
    x, c = s // 2, s % 2
    sx = (s + 2) % 4
    sib = s + 1 - 2 * c
    to_x, to_y, to_c = {"samples": sx}, {"groups": 1 - y}, {"samples": sib}
    to_d = {"groups": 1 - y, "samples": sx}
    block = cm.shape[3]
    share = cm.shape[2]
    left, right = slice(0, block // 2), slice(block // 2, block)
    piece = share // 8
    lanes = anc.shape[1]
    w = lanes // n

    barrier = pltpu.get_barrier_semaphore()
    peers = [{"rows": (z + k) % n} for k in range(1, n)] + [to_d, to_x, to_y, to_c]
    for peer in peers:
        pl.semaphore_signal(barrier, inc=1, device_id=peer, device_id_type=pl.DeviceIdType.MESH)

    local = [
        pltpu.make_async_copy(rm_h, rm, loc.at[0]),
        pltpu.make_async_copy(anc_h, anc, loc.at[1]),
        pltpu.make_async_copy(pan_h, pk.at[:, :, s], loc.at[2]),
        pltpu.make_async_copy(off_h, off, loc.at[3]),
        pltpu.make_async_copy(crs_h, cm.at[:, z], loc.at[5]),
        pltpu.make_async_copy(noise_h, nz, loc.at[4]),
    ]
    for g in (0, 1):
        for ref, at, side in (
            (inv_h.at[2 * g : 2 * g + 2], 0, left), (inv_h.at[2 * g : 2 * g + 2], 2, right),
            (lnk_h.at[g : g + 1], 4, left), (lnk_h.at[g : g + 1], 5, right),
        ):
            size = 2 if at < 4 else 1
            local.append(pltpu.make_async_copy(ref.at[:, :, side], tm.at[g, at : at + size, z], loc.at[6]))
    for copy in local[:2]:
        copy.start()

    def remote(src, dst, ss, rs, where):
        return pltpu.make_async_remote_copy(
            src_ref=src, dst_ref=dst, send_sem=ss, recv_sem=rs,
            device_id=where, device_id_type=pl.DeviceIdType.MESH,
        )

    def go(src, dst, ss, rs, where):
        remote(src, dst, sent.at[ss], rs, where).start()

    def whole(ref, sem):
        pltpu.make_async_copy(ref, ref, sem).wait()

    def rows_at(index, size):
        return pl.ds(pl.multiple_of(index * size, size), size)

    q = c * 4 + x * 2 + y
    def by(index, make):
        pl.when(index < n // 2)(lambda: make(0))
        pl.when(index >= n // 2)(lambda: make(2))

    def send_z(g):
        own = rows_at(q, piece)

        def make(low):
            for k in range(1, n):
                where = {"rows": (z + k) % n}
                pair = inv_h.at[2 * g : 2 * g + 2, own]
                if low == 0:
                    go(pair.at[:, :, left], tm.at[g, 0:2, z, own], 1, zr.at[g, k], where)
                go(pair.at[:, :, right], tm.at[g, 2:4, z, own], 1, zr.at[g, k], where)
                one = lnk_h.at[g : g + 1, own]
                go(one.at[:, :, left], tm.at[g, 4:5, z, own], 1, zr.at[g, k], where)
                go(one.at[:, :, right], tm.at[g, 5:6, z, own], 1, zr.at[g, k], where)

        if g < 2:
            by(z, make)
        else:
            for k in range(1, n):
                go(crs_h.at[:, own], cm.at[:, z, own], 7, zr.at[g, k], {"rows": (z + k) % n})

    def send_p(p):
        for b in (1, 0):
            go(pan_h.at[p, b], pk.at[p, b, s], 0, pxr.at[p, b], to_x)
        go(pan_h.at[p], pk.at[p, :, s], 0, pcr.at[p], to_c)

    def relay_p(p, b):
        whole(pk.at[p, b, sx], pxr.at[p, b])
        go(pk.at[p, b, sx], pk.at[p, b, sx], 0, prr.at[p, b], to_c)

    def sibling_p(p):
        whole(pk.at[p, :, sib], pcr.at[p])

    def relayed_p(p, b):
        whole(pk.at[p, b, sib], prr.at[p, b])

    def gather(p):
        def rows8(i, carry):
            for r in range(8):
                fr[p, pl.ds(i * 8 + r, 1), :] = anc[pl.ds(rm[p, i * 8 + r], 1), :]
            return carry

        lax.fori_loop(0, fr.shape[1] // 8, rows8, 0)

    def spread(g):
        for k in range(1, n):
            zz = (z + n - k) % n

            def make(low):
                ref = tm.at[g, low:6, zz, rows_at(q, piece)] if g < 2 else cm.at[:, zz, rows_at(q, piece)]
                whole(ref, zr.at[g, k])
                for where in (to_d, to_x, to_y):
                    go(ref, ref, 5 if g < 2 else 7, mr.at[g, k], where)

            by(zz, make) if g < 2 else make(0)

    def join(g):
        for k in range(1, n):
            zz = (z + n - k) % n

            def make(low):
                whole(tm.at[g, low:6, zz, 0 : 3 * piece] if g < 2 else cm.at[:, zz, 0 : 3 * piece], mr.at[g, k])
                own = rows_at(c, 4 * piece)
                ref = tm.at[g, low:6, zz, own] if g < 2 else cm.at[:, zz, own]
                go(ref, ref, 6 if g < 2 else 7, cr.at[g], to_c)

            by(zz, make) if g < 2 else make(0)

    def joined(g):
        if g < 2:
            by(z, lambda low: whole(tm.at[g, 0:4, 0:2, 0 : (7 + low // 2) * piece], cr.at[g]))
        else:
            whole(cm.at[:, 0 : n - 1, 0 : 4 * piece], cr.at[g])

    def matrix(g, i):
        return jnp.concatenate(
            [tm[g, at].reshape(block, block // 2) for at in ((i, i + 2) if i < 2 else (4, 5))], axis=1
        )

    def sums_1(b, fh, fb):
        ph, low = split(pk[1, b].reshape(block, block))
        both = dot(fb, ph, NT)
        y1[b] = both[:lanes] + (both[lanes:] + dot(fh, low, NT))
        for k in range(1, n):
            zz = (z + k) % n
            go(y1.at[b, rows_at(zz, w)], r1.at[k, b], 2, ar.at[b], {"rows": zz})

    def sums_0(b, value):
        y0[b] = value
        for k in range(1, n):
            zz = (z + k) % n
            go(y0.at[b, rows_at(zz, share)], r0.at[k, b], 3, br.at[b], {"rows": zz})

    def residue(b):
        whole(r1.at[1:n, b], ar.at[b])
        total = y1[b, rows_at(z, w), :]
        for k in range(1, n):
            total = total + r1[k, b]
        return tt[rows_at(z, w), b * block : (b + 1) * block] - total

    def back(p, first, second):
        for i in range(n):
            cut = slice(i * share, (i + 1) * share)
            osend[p, i] = jnp.concatenate([first[:, cut], second[:, cut]], axis=1)
        orecv[p, z] = osend[p, z]
        for k in range(1, n):
            zz = (z + k) % n
            go(osend.at[p, zz], orecv.at[p, z], 4, osr.at[p], {"rows": zz})

    def landed(p):
        whole(orecv.at[p, 0 : n - 1], osr.at[p])
        return orecv[p].reshape(lanes, 2 * share).T.reshape(2, share, lanes)

    pl.semaphore_wait(barrier, len(peers))
    send_p(1)
    send_z(0)
    local[2].start()
    send_p(0)
    send_z(1)
    send_z(2)
    for g in (0, 1):
        tm[g, 0:2, n // 2 : n] = jnp.zeros((2, n - n // 2, share, block // 2), F32)
    for copy in local[3:]:
        copy.start()

    local[0].wait()
    local[1].wait()
    gather(1)
    fh, low = split(fr[1].T)
    fb = jnp.concatenate([fh, low], 0)
    relay_p(1, 1)
    relay_p(1, 0)
    spread(0)
    local[2].wait()
    sibling_p(1)
    relayed_p(1, 1)
    sums_1(1, fh, fb)
    relayed_p(1, 0)
    sums_1(0, fh, fb)
    gather(0)
    relay_p(0, 1)
    relay_p(0, 0)
    spread(1)
    local[3].wait()
    whole(cm.at[:, z], loc.at[5])
    whole(tm.at[:, :, z], loc.at[6])
    local[5].wait()
    sibling_p(0)
    rest = {}
    for b in (1, 0):
        relayed_p(0, b)
        rest[b] = nz[pl.ds(off[0] + b * block, block), :] * (1.0 / n) - mm(pk[0, b].reshape(block, block), fr[0], NN)
    spread(2)
    tt[...] = nz[pl.ds(off[1], 2 * block), :].T
    join(0)
    joined(0)
    part = mm(matrix(0, 1), rest[1], NN)
    sums_0(1, part)
    sums_0(0, mm(matrix(0, 0), rest[0] - mm(matrix(0, 2).T, part, NN), NN))
    join(1)
    joined(1)
    s11 = mm(residue(1), matrix(1, 1), NT)
    s10 = mm(residue(0) - mm(s11, matrix(1, 2), NN), matrix(1, 0), NT)
    back(1, s10, s11)
    join(2)
    joined(2)
    s1 = jnp.concatenate([s10, s11], axis=1)
    v01 = mm(-mm(s1, cm[2:4].reshape(2 * block, block), NN), matrix(0, 1), NT)
    v00 = mm(-(mm(s1, cm[0:2].reshape(2 * block, block), NN) + mm(v01, matrix(0, 2), NN)), matrix(0, 0), NT)
    back(0, v00, v01)
    out[1] = landed(1)
    total = []
    for b in (0, 1):
        whole(r0.at[1:n, b], br.at[b])
        own = y0[b, rows_at(z, share), :]
        for k in range(1, n):
            own = own + r0[k, b]
        total.append(own)
    last = landed(0)
    for b in (0, 1):
        out[0, b] = last[b] + total[b]
    whole(pk.at[:, :, 0:3], sent.at[0])
    whole(cm.at[:, 0 : n - 1], sent.at[7])

    def finish(low):
        size = (7 + low // 2) * piece
        whole(tm.at[:, low:6, 0 : n - 1, 0:piece], sent.at[1])
        whole(tm.at[:, :, 0, 0:size], sent.at[5])
        whole(tm.at[:, 0:4, 0:2, 0:size], sent.at[6])

    by(z, finish)
    whole(r1.at[1:n], sent.at[2])
    whole(r0.at[1:n], sent.at[3])
    whole(orecv.at[:, 0 : n - 1], sent.at[4])


def fused(n, ancestor, panels, row_map, offsets, noise, inverse, inner_link, cross_link):
    share, block = inverse.shape[2:]
    lanes = ancestor.shape[1]
    w = lanes // n
    cols, rows = panels.shape[3], panels.shape[2]
    dma = pltpu.SemaphoreType.DMA
    hbm = pl.BlockSpec(memory_space=pltpu.HBM)
    args = (
        row_map, offsets, ancestor, jnp.swapaxes(panels, 2, 3), noise,
        inverse.reshape(4, share, block), inner_link, cross_link.reshape(4, share, block),
    )
    return pl.pallas_call(
        functools.partial(kernel, n),
        name="substitute",
        out_shape=jax.ShapeDtypeStruct((2, 2, share, lanes), F32),
        in_specs=[hbm] * 8,
        out_specs=pl.BlockSpec(memory_space=pltpu.VMEM),
        scratch_shapes=[
            pltpu.SMEM(row_map.shape, jnp.int32),
            pltpu.SMEM(offsets.shape, jnp.int32),
            pltpu.VMEM(ancestor.shape, F32),
            pltpu.VMEM(noise.shape, F32),
            pltpu.VMEM((2, 6, n, share, block // 2), F32),
            pltpu.VMEM((4, n, share, block), F32),
            pltpu.VMEM((2, 2, 4, cols, rows), F32),
            pltpu.VMEM((2, rows, lanes), F32),
            pltpu.VMEM((lanes, 2 * block), F32),
            pltpu.VMEM((2, lanes, block), F32),
            pltpu.VMEM((2, block, lanes), F32),
            pltpu.VMEM((n, 2, w, block), F32),
            pltpu.VMEM((n, 2, share, lanes), F32),
            pltpu.VMEM((2, n, w, 2 * share), F32),
            pltpu.VMEM((2, n, w, 2 * share), F32),
            dma((7,)), dma((8,)),
            dma((2, 2)), dma((2,)), dma((2, 2)),
            dma((3, n)), dma((3, n)), dma((3,)),
            dma((2,)), dma((2,)), dma((2,)),
        ],
        compiler_params=pltpu.CompilerParams(
            collective_id=0, has_side_effects=True, vmem_limit_bytes=40 * 1024 * 1024
        ),
    )(*[pltpu.with_memory_space_constraint(a, pltpu.HBM) for a in args])


def solution(mesh):
    placed = (
        P(("groups", "rows"), "samples"),
        P(None, None, "rows", "samples"),
        P(None, "rows"),
        P(),
        P("groups", "samples"),
        P(None, None, "rows", None),
        P(None, "rows", None),
        P(None, None, "rows", None),
    )
    n = mesh.shape["rows"]

    def local(ancestor, panels, row_map, offsets, noise, inverse, inner_link, cross_link):
        args = (ancestor, panels, row_map, offsets, noise, inverse, inner_link, cross_link)
        fits = (
            mesh.shape["groups"] == 2
            and mesh.shape["samples"] == 4
            and n == 4
            and ancestor.shape[1] == 128
            and inverse.shape[2] % 64 == 0
            and inverse.shape[3] == n * inverse.shape[2]
            and row_map.shape[1] % 128 == 0
        )
        return fused(n, *args) if fits else plain(*args)

    return jax.shard_map(
        local,
        mesh=mesh,
        in_specs=placed,
        out_specs=P(None, None, "rows", ("groups", "samples")),
        check_vma=False,
    )
```

```python
import functools

import jax
import jax.numpy as jnp
from jax import lax
from jax.experimental import pallas as pl
from jax.experimental.pallas import tpu as pltpu
from jax.sharding import PartitionSpec as P

F32 = jnp.float32
BF16 = jnp.bfloat16
NN = ((1,), (0,))
NT = ((1,), (1,))


def product(left, right):
    return jnp.dot(left, right, precision=lax.Precision.HIGHEST, preferred_element_type=F32)


def apply_inverse(target, partial_value, inverse_rows):
    rows_here = inverse_rows.shape[0]
    share = lax.psum_scatter(partial_value, "rows", scatter_dimension=0, tiled=True)
    first_own = lax.axis_index("rows") * rows_here
    residue = lax.dynamic_slice_in_dim(target, first_own, rows_here, 0) - share
    return product(inverse_rows, lax.all_gather(residue, "rows", axis=0, tiled=True))


def plain(ancestor, panels, row_map, offsets, noise, inverse, inner_link, cross_link):
    block_rows = inverse.shape[3]
    solved = [[None, None], [None, None]]
    for p in (1, 0):
        front_rows = jnp.take(ancestor, row_map[p], axis=0)
        window = lax.dynamic_slice_in_dim(noise, offsets[p], 2 * block_rows, 0)
        for b in (1, 0):
            whole = lax.all_gather(panels[p, b], "samples", axis=1, tiled=True)
            partial_value = product(whole.T, front_rows)
            if b == 0:
                partial_value = partial_value + product(inner_link[p].T, solved[p][1])
            if p == 0:
                for e in (0, 1):
                    partial_value = partial_value + product(cross_link[b, e].T, solved[1][e])
            target = window[b * block_rows : (b + 1) * block_rows]
            solved[p][b] = apply_inverse(target, partial_value, inverse[p, b])
    return jnp.stack([jnp.stack(solved[0]), jnp.stack(solved[1])])


def split(a):
    hi = a.astype(BF16)
    return hi, (a - hi.astype(F32)).astype(BF16)


def dot(a, b, dims):
    return lax.dot_general(a, b, (dims, ((), ())), preferred_element_type=F32)


def mm(a, b, dims):
    ah, al = split(a)
    bh, bl = split(b)
    m = a.shape[0]
    both = dot(jnp.concatenate([ah, al], 0), bh, dims)
    return both[:m] + (both[m:] + dot(ah, bl, dims))


def mm_split(a, pair, dims):
    ah, al = split(a)
    bh, bl = pair
    m = a.shape[0]
    both = dot(jnp.concatenate([ah, al], 0), bh, dims)
    return both[:m] + (both[m:] + dot(ah, bl, dims))


def kernel(
    n, rm_h, off_h, anc_h, pan_h, noise_h, inv_h, lnk_h, crs_h, out,
    rm, off, anc, nz, tm, cm, pk, fr, tt, y1, y0, r1, r0, osend, orecv,
    loc, sent, pxr, pcr, prr, zr, mr, cr, ar, br, osr,
):
    y = lax.axis_index("groups")
    z = lax.axis_index("rows")
    s = lax.axis_index("samples")
    x, c = s // 2, s % 2
    sx = (s + 2) % 4
    sib = s + 1 - 2 * c
    to_x, to_y, to_c = {"samples": sx}, {"groups": 1 - y}, {"samples": sib}
    to_d = {"groups": 1 - y, "samples": sx}
    block = cm.shape[3]
    share = cm.shape[2]
    left, right = slice(0, block // 2), slice(block // 2, block)
    piece = share // 8
    lanes = anc.shape[1]
    w = lanes // n

    barrier = pltpu.get_barrier_semaphore()
    peers = [{"rows": (z + k) % n} for k in range(1, n)] + [to_d, to_x, to_y, to_c]
    for peer in peers:
        pl.semaphore_signal(barrier, inc=1, device_id=peer, device_id_type=pl.DeviceIdType.MESH)

    local = [
        pltpu.make_async_copy(rm_h, rm, loc.at[0]),
        pltpu.make_async_copy(anc_h, anc, loc.at[1]),
        pltpu.make_async_copy(pan_h, pk.at[:, :, s], loc.at[2]),
        pltpu.make_async_copy(off_h, off, loc.at[3]),
        pltpu.make_async_copy(crs_h, cm.at[:, z], loc.at[5]),
        pltpu.make_async_copy(noise_h, nz, loc.at[4]),
    ]
    for g in (0, 1):
        for ref, at, side in (
            (inv_h.at[2 * g : 2 * g + 2], 0, left), (inv_h.at[2 * g : 2 * g + 2], 2, right),
            (lnk_h.at[g : g + 1], 4, left), (lnk_h.at[g : g + 1], 5, right),
        ):
            size = 2 if at < 4 else 1
            local.append(pltpu.make_async_copy(ref.at[:, :, side], tm.at[g, at : at + size, z], loc.at[6]))
    for copy in local[:2]:
        copy.start()

    def remote(src, dst, ss, rs, where):
        return pltpu.make_async_remote_copy(
            src_ref=src, dst_ref=dst, send_sem=ss, recv_sem=rs,
            device_id=where, device_id_type=pl.DeviceIdType.MESH,
        )

    def go(src, dst, ss, rs, where):
        remote(src, dst, sent.at[ss], rs, where).start()

    def whole(ref, sem):
        pltpu.make_async_copy(ref, ref, sem).wait()

    def rows_at(index, size):
        return pl.ds(pl.multiple_of(index * size, size), size)

    q = c * 4 + x * 2 + y
    def by(index, make):
        pl.when(index < n // 2)(lambda: make(0))
        pl.when(index >= n // 2)(lambda: make(2))

    def send_z(g):
        own = rows_at(q, piece)

        def make(low):
            for k in range(1, n):
                where = {"rows": (z + k) % n}
                pair = inv_h.at[2 * g : 2 * g + 2, own]
                if low == 0:
                    go(pair.at[:, :, left], tm.at[g, 0:2, z, own], 1, zr.at[g, k], where)
                go(pair.at[:, :, right], tm.at[g, 2:4, z, own], 1, zr.at[g, k], where)
                one = lnk_h.at[g : g + 1, own]
                go(one.at[:, :, left], tm.at[g, 4:5, z, own], 1, zr.at[g, k], where)
                go(one.at[:, :, right], tm.at[g, 5:6, z, own], 1, zr.at[g, k], where)

        if g < 2:
            by(z, make)
        else:
            for k in range(1, n):
                go(crs_h.at[:, own], cm.at[:, z, own], 7, zr.at[g, k], {"rows": (z + k) % n})

    def send_p(p):
        for b in (1, 0):
            go(pan_h.at[p, b], pk.at[p, b, s], 0, pxr.at[p, b], to_x)
        go(pan_h.at[p], pk.at[p, :, s], 0, pcr.at[p], to_c)

    def relay_p(p, b):
        whole(pk.at[p, b, sx], pxr.at[p, b])
        go(pk.at[p, b, sx], pk.at[p, b, sx], 0, prr.at[p, b], to_c)

    def sibling_p(p):
        whole(pk.at[p, :, sib], pcr.at[p])

    def relayed_p(p, b):
        whole(pk.at[p, b, sib], prr.at[p, b])

    def gather(p):
        def rows8(i, carry):
            for r in range(8):
                fr[p, pl.ds(i * 8 + r, 1), :] = anc[pl.ds(rm[p, i * 8 + r], 1), :]
            return carry

        lax.fori_loop(0, fr.shape[1] // 8, rows8, 0)

    def spread(g):
        for k in range(1, n):
            zz = (z + n - k) % n

            def make(low):
                ref = tm.at[g, low:6, zz, rows_at(q, piece)] if g < 2 else cm.at[:, zz, rows_at(q, piece)]
                whole(ref, zr.at[g, k])
                for where in (to_d, to_x, to_y):
                    go(ref, ref, 5 if g < 2 else 7, mr.at[g, k], where)

            by(zz, make) if g < 2 else make(0)

    def join(g):
        for k in range(1, n):
            zz = (z + n - k) % n

            def make(low):
                whole(tm.at[g, low:6, zz, 0 : 3 * piece] if g < 2 else cm.at[:, zz, 0 : 3 * piece], mr.at[g, k])
                own = rows_at(c, 4 * piece)
                ref = tm.at[g, low:6, zz, own] if g < 2 else cm.at[:, zz, own]
                go(ref, ref, 6 if g < 2 else 7, cr.at[g], to_c)

            by(zz, make) if g < 2 else make(0)

    def joined(g):
        if g < 2:
            by(z, lambda low: whole(tm.at[g, 0:4, 0:2, 0 : (7 + low // 2) * piece], cr.at[g]))
        else:
            whole(cm.at[:, 0 : n - 1, 0 : 4 * piece], cr.at[g])

    def matrix(g, i):
        return jnp.concatenate(
            [tm[g, at].reshape(block, block // 2) for at in ((i, i + 2) if i < 2 else (4, 5))], axis=1
        )

    def sums_1(b, fh, fb):
        ph, low = split(pk[1, b].reshape(block, block))
        both = dot(fb, ph, NT)
        y1[b] = both[:lanes] + (both[lanes:] + dot(fh, low, NT))
        for k in range(1, n):
            zz = (z + k) % n
            go(y1.at[b, rows_at(zz, w)], r1.at[k, b], 2, ar.at[b], {"rows": zz})

    def sums_0(b, value):
        y0[b] = value
        for k in range(1, n):
            zz = (z + k) % n
            go(y0.at[b, rows_at(zz, share)], r0.at[k, b], 3, br.at[b], {"rows": zz})

    def residue(b):
        whole(r1.at[1:n, b], ar.at[b])
        total = y1[b, rows_at(z, w), :]
        for k in range(1, n):
            total = total + r1[k, b]
        return tt[rows_at(z, w), b * block : (b + 1) * block] - total

    def back(p, first, second):
        for i in range(n):
            cut = slice(i * share, (i + 1) * share)
            osend[p, i] = jnp.concatenate([first[:, cut], second[:, cut]], axis=1)
        orecv[p, z] = osend[p, z]
        for k in range(1, n):
            zz = (z + k) % n
            go(osend.at[p, zz], orecv.at[p, z], 4, osr.at[p], {"rows": zz})

    def landed(p):
        whole(orecv.at[p, 0 : n - 1], osr.at[p])
        return orecv[p].reshape(lanes, 2 * share).T.reshape(2, share, lanes)

    pl.semaphore_wait(barrier, len(peers))
    send_p(1)
    send_z(0)
    local[2].start()
    send_p(0)
    send_z(1)
    send_z(2)
    for g in (0, 1):
        tm[g, 0:2, n // 2 : n] = jnp.zeros((2, n - n // 2, share, block // 2), F32)
    for copy in local[3:]:
        copy.start()

    local[0].wait()
    local[1].wait()
    gather(1)
    fh, low = split(fr[1].T)
    fb = jnp.concatenate([fh, low], 0)
    relay_p(1, 1)
    relay_p(1, 0)
    spread(0)
    local[2].wait()
    sibling_p(1)
    relayed_p(1, 1)
    sums_1(1, fh, fb)
    relayed_p(1, 0)
    sums_1(0, fh, fb)
    gather(0)
    relay_p(0, 1)
    relay_p(0, 0)
    spread(1)
    local[3].wait()
    whole(cm.at[:, z], loc.at[5])
    whole(tm.at[:, :, z], loc.at[6])
    local[5].wait()
    sibling_p(0)
    rest = {}
    for b in (1, 0):
        relayed_p(0, b)
        rest[b] = nz[pl.ds(off[0] + b * block, block), :] * (1.0 / n) - mm(pk[0, b].reshape(block, block), fr[0], NN)
    spread(2)
    tt[...] = nz[pl.ds(off[1], 2 * block), :].T
    join(0)
    joined(0)
    part = mm(matrix(0, 1), rest[1], NN)
    sums_0(1, part)
    sums_0(0, mm(matrix(0, 0), rest[0] - mm(matrix(0, 2).T, part, NN), NN))
    joined_inverse = mm(matrix(0, 0), mm(matrix(0, 2).T, matrix(0, 1), NN), NN)
    inv_00, inv_01, inv_mid = split(matrix(0, 0)), split(matrix(0, 1)), split(joined_inverse)
    join(1)
    joined(1)
    s11 = mm(residue(1), matrix(1, 1), NT)
    s10 = mm(residue(0) - mm(s11, matrix(1, 2), NN), matrix(1, 0), NT)
    back(1, s10, s11)
    join(2)
    joined(2)
    s1 = jnp.concatenate([s10, s11], axis=1)
    u0 = mm(s1, cm[0:2].reshape(2 * block, block), NN)
    u1 = mm(s1, cm[2:4].reshape(2 * block, block), NN)
    v00 = mm_split(u1, inv_mid, NT) - mm_split(u0, inv_00, NT)
    v01 = -mm_split(u1, inv_01, NT)
    back(0, v00, v01)
    out[1] = landed(1)
    total = []
    for b in (0, 1):
        whole(r0.at[1:n, b], br.at[b])
        own = y0[b, rows_at(z, share), :]
        for k in range(1, n):
            own = own + r0[k, b]
        total.append(own)
    last = landed(0)
    for b in (0, 1):
        out[0, b] = last[b] + total[b]
    whole(pk.at[:, :, 0:3], sent.at[0])
    whole(cm.at[:, 0 : n - 1], sent.at[7])

    def finish(low):
        size = (7 + low // 2) * piece
        whole(tm.at[:, low:6, 0 : n - 1, 0:piece], sent.at[1])
        whole(tm.at[:, :, 0, 0:size], sent.at[5])
        whole(tm.at[:, 0:4, 0:2, 0:size], sent.at[6])

    by(z, finish)
    whole(r1.at[1:n], sent.at[2])
    whole(r0.at[1:n], sent.at[3])
    whole(orecv.at[:, 0 : n - 1], sent.at[4])


def fused(n, ancestor, panels, row_map, offsets, noise, inverse, inner_link, cross_link):
    share, block = inverse.shape[2:]
    lanes = ancestor.shape[1]
    w = lanes // n
    cols, rows = panels.shape[3], panels.shape[2]
    dma = pltpu.SemaphoreType.DMA
    hbm = pl.BlockSpec(memory_space=pltpu.HBM)
    args = (
        row_map, offsets, ancestor, jnp.swapaxes(panels, 2, 3), noise,
        inverse.reshape(4, share, block), inner_link, cross_link.reshape(4, share, block),
    )
    return pl.pallas_call(
        functools.partial(kernel, n),
        name="substitute",
        out_shape=jax.ShapeDtypeStruct((2, 2, share, lanes), F32),
        in_specs=[hbm] * 8,
        out_specs=pl.BlockSpec(memory_space=pltpu.VMEM),
        scratch_shapes=[
            pltpu.SMEM(row_map.shape, jnp.int32),
            pltpu.SMEM(offsets.shape, jnp.int32),
            pltpu.VMEM(ancestor.shape, F32),
            pltpu.VMEM(noise.shape, F32),
            pltpu.VMEM((2, 6, n, share, block // 2), F32),
            pltpu.VMEM((4, n, share, block), F32),
            pltpu.VMEM((2, 2, 4, cols, rows), F32),
            pltpu.VMEM((2, rows, lanes), F32),
            pltpu.VMEM((lanes, 2 * block), F32),
            pltpu.VMEM((2, lanes, block), F32),
            pltpu.VMEM((2, block, lanes), F32),
            pltpu.VMEM((n, 2, w, block), F32),
            pltpu.VMEM((n, 2, share, lanes), F32),
            pltpu.VMEM((2, n, w, 2 * share), F32),
            pltpu.VMEM((2, n, w, 2 * share), F32),
            dma((7,)), dma((8,)),
            dma((2, 2)), dma((2,)), dma((2, 2)),
            dma((3, n)), dma((3, n)), dma((3,)),
            dma((2,)), dma((2,)), dma((2,)),
        ],
        compiler_params=pltpu.CompilerParams(
            collective_id=0, has_side_effects=True, vmem_limit_bytes=40 * 1024 * 1024
        ),
    )(*[pltpu.with_memory_space_constraint(a, pltpu.HBM) for a in args])


def solution(mesh):
    placed = (
        P(("groups", "rows"), "samples"),
        P(None, None, "rows", "samples"),
        P(None, "rows"),
        P(),
        P("groups", "samples"),
        P(None, None, "rows", None),
        P(None, "rows", None),
        P(None, None, "rows", None),
    )
    n = mesh.shape["rows"]

    def local(ancestor, panels, row_map, offsets, noise, inverse, inner_link, cross_link):
        args = (ancestor, panels, row_map, offsets, noise, inverse, inner_link, cross_link)
        fits = (
            mesh.shape["groups"] == 2
            and mesh.shape["samples"] == 4
            and n == 4
            and ancestor.shape[1] == 128
            and inverse.shape[2] % 64 == 0
            and inverse.shape[3] == n * inverse.shape[2]
            and row_map.shape[1] % 128 == 0
        )
        return fused(n, *args) if fits else plain(*args)

    return jax.shard_map(
        local,
        mesh=mesh,
        in_specs=placed,
        out_specs=P(None, None, "rows", ("groups", "samples")),
        check_vma=False,
    )
```

```python
import functools

import jax
import jax.numpy as jnp
from jax import lax
from jax.experimental import pallas as pl
from jax.experimental.pallas import tpu as pltpu
from jax.sharding import PartitionSpec as P

F32 = jnp.float32
BF16 = jnp.bfloat16
NN = ((1,), (0,))
NT = ((1,), (1,))


def product(left, right):
    return jnp.dot(left, right, precision=lax.Precision.HIGHEST, preferred_element_type=F32)


def apply_inverse(target, partial_value, inverse_rows):
    rows_here = inverse_rows.shape[0]
    share = lax.psum_scatter(partial_value, "rows", scatter_dimension=0, tiled=True)
    first_own = lax.axis_index("rows") * rows_here
    residue = lax.dynamic_slice_in_dim(target, first_own, rows_here, 0) - share
    return product(inverse_rows, lax.all_gather(residue, "rows", axis=0, tiled=True))


def plain(ancestor, panels, row_map, offsets, noise, inverse, inner_link, cross_link):
    block_rows = inverse.shape[3]
    solved = [[None, None], [None, None]]
    for p in (1, 0):
        front_rows = jnp.take(ancestor, row_map[p], axis=0)
        window = lax.dynamic_slice_in_dim(noise, offsets[p], 2 * block_rows, 0)
        for b in (1, 0):
            whole = lax.all_gather(panels[p, b], "samples", axis=1, tiled=True)
            partial_value = product(whole.T, front_rows)
            if b == 0:
                partial_value = partial_value + product(inner_link[p].T, solved[p][1])
            if p == 0:
                for e in (0, 1):
                    partial_value = partial_value + product(cross_link[b, e].T, solved[1][e])
            target = window[b * block_rows : (b + 1) * block_rows]
            solved[p][b] = apply_inverse(target, partial_value, inverse[p, b])
    return jnp.stack([jnp.stack(solved[0]), jnp.stack(solved[1])])


def split(a):
    hi = a.astype(BF16)
    return hi, (a - hi.astype(F32)).astype(BF16)


def dot(a, b, dims):
    return lax.dot_general(a, b, (dims, ((), ())), preferred_element_type=F32)


def mm(a, b, dims):
    ah, al = split(a)
    bh, bl = split(b)
    m = a.shape[0]
    both = dot(jnp.concatenate([ah, al], 0), bh, dims)
    return both[:m] + (both[m:] + dot(ah, bl, dims))


def mm_split(a, pair, dims):
    ah, al = split(a)
    bh, bl = pair
    m = a.shape[0]
    both = dot(jnp.concatenate([ah, al], 0), bh, dims)
    return both[:m] + (both[m:] + dot(ah, bl, dims))


def kernel(
    n, rm_h, off_h, anc_h, pan_h, noise_h, inv_h, lnk_h, crs_h, out,
    rm, off, anc, nz, tm, cm, pk, fr, tt, y1, y0, r1, r0, osend, orecv,
    loc, sent, pxr, pcr, prr, zr, mr, cr, ar, br, osr,
):
    y = lax.axis_index("groups")
    z = lax.axis_index("rows")
    s = lax.axis_index("samples")
    x, c = s // 2, s % 2
    sx = (s + 2) % 4
    sib = s + 1 - 2 * c
    to_x, to_y, to_c = {"samples": sx}, {"groups": 1 - y}, {"samples": sib}
    to_d = {"groups": 1 - y, "samples": sx}
    block = cm.shape[3]
    share = cm.shape[2]
    left, right = slice(0, block // 2), slice(block // 2, block)
    piece = share // 8
    lanes = anc.shape[1]
    w = lanes // n
    up = [j + (j >= z).astype(jnp.int32) for j in range(n - 1)]

    barrier = pltpu.get_barrier_semaphore()
    peers = [{"rows": (z + k) % n} for k in range(1, n)] + [to_d, to_x, to_y, to_c]
    for peer in peers:
        pl.semaphore_signal(barrier, inc=1, device_id=peer, device_id_type=pl.DeviceIdType.MESH)

    local = [
        pltpu.make_async_copy(rm_h, rm, loc.at[0]),
        pltpu.make_async_copy(anc_h, anc, loc.at[1]),
        pltpu.make_async_copy(pan_h, pk.at[:, :, s], loc.at[2]),
        pltpu.make_async_copy(off_h, off, loc.at[3]),
        pltpu.make_async_copy(crs_h, cm.at[:, z], loc.at[5]),
        pltpu.make_async_copy(noise_h, nz, loc.at[4]),
    ]
    for g in (0, 1):
        for ref, at, side in (
            (inv_h.at[2 * g : 2 * g + 2], 0, left), (inv_h.at[2 * g : 2 * g + 2], 2, right),
            (lnk_h.at[g : g + 1], 4, left), (lnk_h.at[g : g + 1], 5, right),
        ):
            size = 2 if at < 4 else 1
            local.append(pltpu.make_async_copy(ref.at[:, :, side], tm.at[g, at : at + size, z], loc.at[6]))
    for copy in local[:2]:
        copy.start()

    def remote(src, dst, ss, rs, where):
        return pltpu.make_async_remote_copy(
            src_ref=src, dst_ref=dst, send_sem=ss, recv_sem=rs,
            device_id=where, device_id_type=pl.DeviceIdType.MESH,
        )

    def go(src, dst, ss, rs, where):
        remote(src, dst, sent.at[ss], rs, where).start()

    def whole(ref, sem):
        pltpu.make_async_copy(ref, ref, sem).wait()

    def rows_at(index, size):
        return pl.ds(pl.multiple_of(index * size, size), size)

    q = c * 4 + x * 2 + y
    def by(index, make):
        pl.when(index < n // 2)(lambda: make(0))
        pl.when(index >= n // 2)(lambda: make(2))

    def send_z(g):
        own = rows_at(q, piece)

        def make(low):
            for k in range(1, n):
                where = {"rows": (z + k) % n}
                pair = inv_h.at[2 * g : 2 * g + 2, own]
                if low == 0:
                    go(pair.at[:, :, left], tm.at[g, 0:2, z, own], 1, zr.at[g, k - 1], where)
                go(pair.at[:, :, right], tm.at[g, 2:4, z, own], 1, zr.at[g, k - 1], where)
                one = lnk_h.at[g : g + 1, own]
                go(one.at[:, :, left], tm.at[g, 4:5, z, own], 1, zr.at[g, k - 1], where)
                go(one.at[:, :, right], tm.at[g, 5:6, z, own], 1, zr.at[g, k - 1], where)

        if g < 2:
            by(z, make)
        else:
            for k in range(1, n):
                go(crs_h.at[:, own], cm.at[:, z, own], 7, zr.at[g, k - 1], {"rows": (z + k) % n})

    def send_p(p):
        for b in (1, 0):
            go(pan_h.at[p, b], pk.at[p, b, s], 0, pxr.at[p, b], to_x)
        go(pan_h.at[p], pk.at[p, :, s], 0, pcr.at[p], to_c)

    def relay_p(p, b):
        whole(pk.at[p, b, sx], pxr.at[p, b])
        go(pk.at[p, b, sx], pk.at[p, b, sx], 0, prr.at[p, b], to_c)

    def sibling_p(p):
        whole(pk.at[p, :, sib], pcr.at[p])

    def relayed_p(p, b):
        whole(pk.at[p, b, sib], prr.at[p, b])

    def gather(p):
        def rows8(i, carry):
            for r in range(8):
                fr[p, pl.ds(i * 8 + r, 1), :] = anc[pl.ds(rm[p, i * 8 + r], 1), :]
            return carry

        lax.fori_loop(0, fr.shape[1] // 8, rows8, 0)

    def spread(g):
        for k in range(1, n):
            zz = (z + n - k) % n

            def make(low):
                ref = tm.at[g, low:6, zz, rows_at(q, piece)] if g < 2 else cm.at[:, zz, rows_at(q, piece)]
                whole(ref, zr.at[g, k - 1])
                for where in (to_y, to_d, to_x):
                    go(ref, ref, 5 if g < 2 else 7, mr.at[g, k - 1], where)

            by(zz, make) if g < 2 else make(0)

    def join(g):
        for k in range(1, n):
            zz = (z + n - k) % n

            def make(low):
                whole(tm.at[g, low:6, zz, 0 : 3 * piece] if g < 2 else cm.at[:, zz, 0 : 3 * piece], mr.at[g, k - 1])
                own = rows_at(c, 4 * piece)
                ref = tm.at[g, low:6, zz, own] if g < 2 else cm.at[:, zz, own]
                go(ref, ref, 6 if g < 2 else 7, cr.at[g], to_c)

            by(zz, make) if g < 2 else make(0)

    def joined(g):
        if g < 2:
            by(z, lambda low: whole(tm.at[g, 0:4, 0:2, 0 : (7 + low // 2) * piece], cr.at[g]))
        else:
            whole(cm.at[:, 0 : n - 1, 0 : 4 * piece], cr.at[g])

    def matrix(g, i):
        return jnp.concatenate(
            [tm[g, at].reshape(block, block // 2) for at in ((i, i + 2) if i < 2 else (4, 5))], axis=1
        )

    def sums_1(b, fh, fb):
        ph, low = split(pk[1, b].reshape(block, block))
        both = dot(fb, ph, NT)
        y1[b] = both[:lanes] + (both[lanes:] + dot(fh, low, NT))
        for zz in up:
            k = (zz + n - z) % n
            go(y1.at[b, rows_at(zz, w)], r1.at[k, b], 2, ar.at[b], {"rows": zz})

    def sums_0(b, value):
        y0[b] = value
        for zz in up:
            k = (zz + n - z) % n
            go(y0.at[b, rows_at(zz, share)], r0.at[k, b], 3, br.at[b], {"rows": zz})

    def residue(b):
        whole(r1.at[1:n, b], ar.at[b])
        total = y1[b, rows_at(z, w), :]
        for k in range(1, n):
            total = total + r1[k, b]
        return tt[rows_at(z, w), b * block : (b + 1) * block] - total

    def back(p, first, second):
        for i in range(n):
            cut = slice(i * share, (i + 1) * share)
            osend[p, i] = jnp.concatenate([first[:, cut], second[:, cut]], axis=1)
        orecv[p, z] = osend[p, z]
        for zz in up:
            go(osend.at[p, zz], orecv.at[p, z], 4, osr.at[p], {"rows": zz})

    def landed(p):
        whole(orecv.at[p, 0 : n - 1], osr.at[p])
        return orecv[p].reshape(lanes, 2 * share).T.reshape(2, share, lanes)

    pl.semaphore_wait(barrier, len(peers))
    send_p(1)
    send_z(0)
    local[2].start()
    send_p(0)
    send_z(1)
    send_z(2)
    for g in (0, 1):
        tm[g, 0:2, n // 2 : n] = jnp.zeros((2, n - n // 2, share, block // 2), F32)
    for copy in local[3:]:
        copy.start()

    local[0].wait()
    local[1].wait()
    gather(1)
    fh, low = split(fr[1].T)
    fb = jnp.concatenate([fh, low], 0)
    relay_p(1, 1)
    relay_p(1, 0)
    spread(0)
    local[2].wait()
    sibling_p(1)
    relayed_p(1, 1)
    sums_1(1, fh, fb)
    relayed_p(1, 0)
    sums_1(0, fh, fb)
    gather(0)
    relay_p(0, 1)
    relay_p(0, 0)
    spread(1)
    local[3].wait()
    whole(cm.at[:, z], loc.at[5])
    whole(tm.at[:, :, z], loc.at[6])
    local[5].wait()
    sibling_p(0)
    rest = {}
    for b in (1, 0):
        relayed_p(0, b)
        rest[b] = nz[pl.ds(off[0] + b * block, block), :] * (1.0 / n) - mm(pk[0, b].reshape(block, block), fr[0], NN)
    spread(2)
    tt[...] = nz[pl.ds(off[1], 2 * block), :].T
    join(0)
    joined(0)
    part = mm(matrix(0, 1), rest[1], NN)
    sums_0(1, part)
    sums_0(0, mm(matrix(0, 0), rest[0] - mm(matrix(0, 2).T, part, NN), NN))
    joined_inverse = mm(matrix(0, 0), mm(matrix(0, 2).T, matrix(0, 1), NN), NN)
    inv_00, inv_01, inv_mid = split(matrix(0, 0)), split(matrix(0, 1)), split(joined_inverse)
    join(1)
    joined(1)
    s11 = mm(residue(1), matrix(1, 1), NT)
    s10 = mm(residue(0) - mm(s11, matrix(1, 2), NN), matrix(1, 0), NT)
    back(1, s10, s11)
    join(2)
    joined(2)
    s1 = jnp.concatenate([s10, s11], axis=1)
    u0 = mm(s1, cm[0:2].reshape(2 * block, block), NN)
    u1 = mm(s1, cm[2:4].reshape(2 * block, block), NN)
    v00 = mm_split(u1, inv_mid, NT) - mm_split(u0, inv_00, NT)
    v01 = -mm_split(u1, inv_01, NT)
    back(0, v00, v01)
    out[1] = landed(1)
    total = []
    for b in (0, 1):
        whole(r0.at[1:n, b], br.at[b])
        own = y0[b, rows_at(z, share), :]
        for k in range(1, n):
            own = own + r0[k, b]
        total.append(own)
    last = landed(0)
    for b in (0, 1):
        out[0, b] = last[b] + total[b]
    whole(pk.at[:, :, 0:3], sent.at[0])
    whole(cm.at[:, 0 : n - 1], sent.at[7])

    def finish(low):
        size = (7 + low // 2) * piece
        whole(tm.at[:, low:6, 0 : n - 1, 0:piece], sent.at[1])
        whole(tm.at[:, :, 0, 0:size], sent.at[5])
        whole(tm.at[:, 0:4, 0:2, 0:size], sent.at[6])

    by(z, finish)
    whole(r1.at[1:n], sent.at[2])
    whole(r0.at[1:n], sent.at[3])
    whole(orecv.at[:, 0 : n - 1], sent.at[4])


def fused(n, ancestor, panels, row_map, offsets, noise, inverse, inner_link, cross_link):
    share, block = inverse.shape[2:]
    lanes = ancestor.shape[1]
    w = lanes // n
    cols, rows = panels.shape[3], panels.shape[2]
    dma = pltpu.SemaphoreType.DMA
    hbm = pl.BlockSpec(memory_space=pltpu.HBM)
    args = (
        row_map, offsets, ancestor, jnp.swapaxes(panels, 2, 3), noise,
        inverse.reshape(4, share, block), inner_link, cross_link.reshape(4, share, block),
    )
    return pl.pallas_call(
        functools.partial(kernel, n),
        name="substitute",
        out_shape=jax.ShapeDtypeStruct((2, 2, share, lanes), F32),
        in_specs=[hbm] * 8,
        out_specs=pl.BlockSpec(memory_space=pltpu.VMEM),
        scratch_shapes=[
            pltpu.SMEM(row_map.shape, jnp.int32),
            pltpu.SMEM(offsets.shape, jnp.int32),
            pltpu.VMEM(ancestor.shape, F32),
            pltpu.VMEM(noise.shape, F32),
            pltpu.VMEM((2, 6, n, share, block // 2), F32),
            pltpu.VMEM((4, n, share, block), F32),
            pltpu.VMEM((2, 2, 4, cols, rows), F32),
            pltpu.VMEM((2, rows, lanes), F32),
            pltpu.VMEM((lanes, 2 * block), F32),
            pltpu.VMEM((2, lanes, block), F32),
            pltpu.VMEM((2, block, lanes), F32),
            pltpu.VMEM((n, 2, w, block), F32),
            pltpu.VMEM((n, 2, share, lanes), F32),
            pltpu.VMEM((2, n, w, 2 * share), F32),
            pltpu.VMEM((2, n, w, 2 * share), F32),
            dma((7,)), dma((8,)),
            dma((2, 2)), dma((2,)), dma((2, 2)),
            dma((3, n - 1)), dma((3, n - 1)), dma((3,)),
            dma((2,)), dma((2,)), dma((2,)),
        ],
        compiler_params=pltpu.CompilerParams(
            collective_id=0, has_side_effects=True, vmem_limit_bytes=40 * 1024 * 1024
        ),
    )(*[pltpu.with_memory_space_constraint(a, pltpu.HBM) for a in args])


def solution(mesh):
    placed = (
        P(("groups", "rows"), "samples"),
        P(None, None, "rows", "samples"),
        P(None, "rows"),
        P(),
        P("groups", "samples"),
        P(None, None, "rows", None),
        P(None, "rows", None),
        P(None, None, "rows", None),
    )
    n = mesh.shape["rows"]

    def local(ancestor, panels, row_map, offsets, noise, inverse, inner_link, cross_link):
        args = (ancestor, panels, row_map, offsets, noise, inverse, inner_link, cross_link)
        fits = (
            mesh.shape["groups"] == 2
            and mesh.shape["samples"] == 4
            and n == 4
            and ancestor.shape[1] == 128
            and inverse.shape[2] % 64 == 0
            and inverse.shape[3] == n * inverse.shape[2]
            and row_map.shape[1] % 128 == 0
        )
        return fused(n, *args) if fits else plain(*args)

    return jax.shard_map(
        local,
        mesh=mesh,
        in_specs=placed,
        out_specs=P(None, None, "rows", ("groups", "samples")),
        check_vma=False,
    )
```

```python
import functools

import jax
import jax.numpy as jnp
from jax import lax
from jax.experimental import pallas as pl
from jax.experimental.pallas import tpu as pltpu
from jax.sharding import PartitionSpec as P

F32 = jnp.float32
BF16 = jnp.bfloat16
NN = ((1,), (0,))
NT = ((1,), (1,))


def product(left, right):
    return jnp.dot(left, right, precision=lax.Precision.HIGHEST, preferred_element_type=F32)


def apply_inverse(target, partial_value, inverse_rows):
    rows_here = inverse_rows.shape[0]
    share = lax.psum_scatter(partial_value, "rows", scatter_dimension=0, tiled=True)
    first_own = lax.axis_index("rows") * rows_here
    residue = lax.dynamic_slice_in_dim(target, first_own, rows_here, 0) - share
    return product(inverse_rows, lax.all_gather(residue, "rows", axis=0, tiled=True))


def plain(ancestor, panels, row_map, offsets, noise, inverse, inner_link, cross_link):
    block_rows = inverse.shape[3]
    solved = [[None, None], [None, None]]
    for p in (1, 0):
        front_rows = jnp.take(ancestor, row_map[p], axis=0)
        window = lax.dynamic_slice_in_dim(noise, offsets[p], 2 * block_rows, 0)
        for b in (1, 0):
            whole = lax.all_gather(panels[p, b], "samples", axis=1, tiled=True)
            partial_value = product(whole.T, front_rows)
            if b == 0:
                partial_value = partial_value + product(inner_link[p].T, solved[p][1])
            if p == 0:
                for e in (0, 1):
                    partial_value = partial_value + product(cross_link[b, e].T, solved[1][e])
            target = window[b * block_rows : (b + 1) * block_rows]
            solved[p][b] = apply_inverse(target, partial_value, inverse[p, b])
    return jnp.stack([jnp.stack(solved[0]), jnp.stack(solved[1])])


def split(a):
    hi = a.astype(BF16)
    return hi, (a - hi.astype(F32)).astype(BF16)


def dot(a, b, dims):
    return lax.dot_general(a, b, (dims, ((), ())), preferred_element_type=F32)


def mm(a, b, dims):
    ah, al = split(a)
    bh, bl = split(b)
    m = a.shape[0]
    both = dot(jnp.concatenate([ah, al], 0), bh, dims)
    return both[:m] + (both[m:] + dot(ah, bl, dims))


def mm_split(a, pair, dims):
    ah, al = split(a)
    bh, bl = pair
    m = a.shape[0]
    both = dot(jnp.concatenate([ah, al], 0), bh, dims)
    return both[:m] + (both[m:] + dot(ah, bl, dims))


def kernel(
    n, rm_h, off_h, anc_h, pan_h, noise_h, inv_h, lnk_h, crs_h, out,
    rm, off, anc, nz, tm, cm, pk, fr, tt, y1, y0, r1, r0, osend, orecv,
    loc, sent, pxr, pcr, prr, zr, mr, cr, ar, br, osr,
):
    y = lax.axis_index("groups")
    z = lax.axis_index("rows")
    s = lax.axis_index("samples")
    x, c = s // 2, s % 2
    sx = (s + 2) % 4
    sib = s + 1 - 2 * c
    to_x, to_y, to_c = {"samples": sx}, {"groups": 1 - y}, {"samples": sib}
    to_d = {"groups": 1 - y, "samples": sx}
    block = cm.shape[3]
    share = cm.shape[2]
    left, right = slice(0, block // 2), slice(block // 2, block)
    piece = share // 8
    lanes = anc.shape[1]
    w = lanes // n
    up = [j + (j >= z).astype(jnp.int32) for j in range(n - 1)]

    barrier = pltpu.get_barrier_semaphore()
    peers = [{"rows": (z + k) % n} for k in range(1, n)] + [to_d, to_x, to_y, to_c]
    for peer in peers:
        pl.semaphore_signal(barrier, inc=1, device_id=peer, device_id_type=pl.DeviceIdType.MESH)

    local = [
        pltpu.make_async_copy(rm_h, rm, loc.at[0]),
        pltpu.make_async_copy(anc_h, anc, loc.at[1]),
        pltpu.make_async_copy(pan_h, pk.at[:, :, s], loc.at[2]),
        pltpu.make_async_copy(off_h, off, loc.at[3]),
        pltpu.make_async_copy(crs_h, cm.at[:, z], loc.at[5]),
        pltpu.make_async_copy(noise_h, nz, loc.at[4]),
    ]
    for g in (0, 1):
        for ref, at, side in (
            (inv_h.at[2 * g : 2 * g + 2], 0, left), (inv_h.at[2 * g : 2 * g + 2], 2, right),
            (lnk_h.at[g : g + 1], 4, left), (lnk_h.at[g : g + 1], 5, right),
        ):
            size = 2 if at < 4 else 1
            local.append(pltpu.make_async_copy(ref.at[:, :, side], tm.at[g, at : at + size, z], loc.at[6 + g]))
    for g in (0, 1):
        tm[g, 0:2, n // 2 : n] = jnp.zeros((2, n - n // 2, share, block // 2), F32)
    for copy in local[:2] + local[-4:]:
        copy.start()

    def remote(src, dst, ss, rs, where):
        return pltpu.make_async_remote_copy(
            src_ref=src, dst_ref=dst, send_sem=ss, recv_sem=rs,
            device_id=where, device_id_type=pl.DeviceIdType.MESH,
        )

    def go(src, dst, ss, rs, where):
        remote(src, dst, sent.at[ss], rs, where).start()

    def whole(ref, sem):
        pltpu.make_async_copy(ref, ref, sem).wait()

    def rows_at(index, size):
        return pl.ds(pl.multiple_of(index * size, size), size)

    q = c * 4 + x * 2 + y
    def by(index, make):
        pl.when(index < n // 2)(lambda: make(0))
        pl.when(index >= n // 2)(lambda: make(2))

    def send_z(g):
        own = rows_at(q, piece)

        def make(low):
            for k in range(1, n):
                where = {"rows": (z + k) % n}
                if g == 1:
                    ref = tm.at[1, low:6, z, own]
                    go(ref, ref, 1, zr.at[g, k - 1], where)
                    continue
                pair = inv_h.at[2 * g : 2 * g + 2, own]
                if low == 0:
                    go(pair.at[:, :, left], tm.at[g, 0:2, z, own], 1, zr.at[g, k - 1], where)
                go(pair.at[:, :, right], tm.at[g, 2:4, z, own], 1, zr.at[g, k - 1], where)
                one = lnk_h.at[g : g + 1, own]
                go(one.at[:, :, left], tm.at[g, 4:5, z, own], 1, zr.at[g, k - 1], where)
                go(one.at[:, :, right], tm.at[g, 5:6, z, own], 1, zr.at[g, k - 1], where)

        if g < 2:
            by(z, make)
        else:
            for k in range(1, n):
                go(crs_h.at[:, own], cm.at[:, z, own], 7, zr.at[g, k - 1], {"rows": (z + k) % n})

    def send_p(p):
        for b in (1, 0):
            go(pan_h.at[p, b], pk.at[p, b, s], 0, pxr.at[p, b], to_x)
        go(pan_h.at[p], pk.at[p, :, s], 0, pcr.at[p], to_c)

    def relay_p(p, b):
        whole(pk.at[p, b, sx], pxr.at[p, b])
        go(pk.at[p, b, sx], pk.at[p, b, sx], 0, prr.at[p, b], to_c)

    def sibling_p(p):
        whole(pk.at[p, :, sib], pcr.at[p])

    def relayed_p(p, b):
        whole(pk.at[p, b, sib], prr.at[p, b])

    def gather(p):
        def rows8(i, carry):
            for r in range(8):
                fr[p, pl.ds(i * 8 + r, 1), :] = anc[pl.ds(rm[p, i * 8 + r], 1), :]
            return carry

        lax.fori_loop(0, fr.shape[1] // 8, rows8, 0)

    def spread(g):
        for k in range(1, n):
            zz = (z + n - k) % n

            def make(low):
                ref = tm.at[g, low:6, zz, rows_at(q, piece)] if g < 2 else cm.at[:, zz, rows_at(q, piece)]
                whole(ref, zr.at[g, k - 1])
                for where in (to_y, to_d, to_x):
                    go(ref, ref, 5 if g < 2 else 7, mr.at[g, k - 1], where)

            by(zz, make) if g < 2 else make(0)

    def join(g):
        for k in range(1, n):
            zz = (z + n - k) % n

            def make(low):
                whole(tm.at[g, low:6, zz, 0 : 3 * piece] if g < 2 else cm.at[:, zz, 0 : 3 * piece], mr.at[g, k - 1])
                own = rows_at(c, 4 * piece)
                ref = tm.at[g, low:6, zz, own] if g < 2 else cm.at[:, zz, own]
                go(ref, ref, 6 if g < 2 else 7, cr.at[g], to_c)

            by(zz, make) if g < 2 else make(0)

    def joined(g):
        if g < 2:
            by(z, lambda low: whole(tm.at[g, 0:4, 0:2, 0 : (7 + low // 2) * piece], cr.at[g]))
        else:
            whole(cm.at[:, 0 : n - 1, 0 : 4 * piece], cr.at[g])

    def matrix(g, i):
        return jnp.concatenate(
            [tm[g, at].reshape(block, block // 2) for at in ((i, i + 2) if i < 2 else (4, 5))], axis=1
        )

    def sums_1(b, fh, fb):
        ph, low = split(pk[1, b].reshape(block, block))
        both = dot(fb, ph, NT)
        y1[b] = both[:lanes] + (both[lanes:] + dot(fh, low, NT))
        for zz in up:
            k = (zz + n - z) % n
            go(y1.at[b, rows_at(zz, w)], r1.at[k, b], 2, ar.at[b], {"rows": zz})

    def sums_0(b, value):
        y0[b] = value
        for zz in up:
            k = (zz + n - z) % n
            go(y0.at[b, rows_at(zz, share)], r0.at[k, b], 3, br.at[b], {"rows": zz})

    def residue(b):
        whole(r1.at[1:n, b], ar.at[b])
        total = y1[b, rows_at(z, w), :]
        for k in range(1, n):
            total = total + r1[k, b]
        return tt[rows_at(z, w), b * block : (b + 1) * block] - total

    def back(p, first, second):
        for i in range(n):
            cut = slice(i * share, (i + 1) * share)
            osend[p, i] = jnp.concatenate([first[:, cut], second[:, cut]], axis=1)
        orecv[p, z] = osend[p, z]
        for zz in up:
            go(osend.at[p, zz], orecv.at[p, z], 4, osr.at[p], {"rows": zz})

    def landed(p):
        whole(orecv.at[p, 0 : n - 1], osr.at[p])
        return orecv[p].reshape(lanes, 2 * share).T.reshape(2, share, lanes)

    pl.semaphore_wait(barrier, len(peers))
    send_p(1)
    send_z(0)
    local[2].start()
    send_p(0)
    whole(tm.at[1, :, z], loc.at[7])
    send_z(1)
    send_z(2)
    for copy in local[3:-4]:
        copy.start()

    relay_p(1, 1)
    local[0].wait()
    local[1].wait()
    gather(1)
    fh, low = split(fr[1].T)
    fb = jnp.concatenate([fh, low], 0)
    relay_p(1, 0)
    spread(0)
    local[2].wait()
    sibling_p(1)
    relayed_p(1, 1)
    sums_1(1, fh, fb)
    relayed_p(1, 0)
    sums_1(0, fh, fb)
    gather(0)
    relay_p(0, 1)
    relay_p(0, 0)
    spread(1)
    local[3].wait()
    whole(cm.at[:, z], loc.at[5])
    whole(tm.at[0, :, z], loc.at[6])
    local[5].wait()
    sibling_p(0)
    rest = {}
    for b in (1, 0):
        relayed_p(0, b)
        rest[b] = nz[pl.ds(off[0] + b * block, block), :] * (1.0 / n) - mm(pk[0, b].reshape(block, block), fr[0], NN)
    spread(2)
    tt[...] = nz[pl.ds(off[1], 2 * block), :].T
    join(0)
    joined(0)
    part = mm(matrix(0, 1), rest[1], NN)
    sums_0(1, part)
    sums_0(0, mm(matrix(0, 0), rest[0] - mm(matrix(0, 2).T, part, NN), NN))
    joined_inverse = mm(matrix(0, 0), mm(matrix(0, 2).T, matrix(0, 1), NN), NN)
    inv_00, inv_01, inv_mid = split(matrix(0, 0)), split(matrix(0, 1)), split(joined_inverse)
    join(1)
    joined(1)
    s11 = mm(residue(1), matrix(1, 1), NT)
    s10 = mm(residue(0) - mm(s11, matrix(1, 2), NN), matrix(1, 0), NT)
    back(1, s10, s11)
    join(2)
    joined(2)
    s1 = jnp.concatenate([s10, s11], axis=1)
    u0 = mm(s1, cm[0:2].reshape(2 * block, block), NN)
    u1 = mm(s1, cm[2:4].reshape(2 * block, block), NN)
    v00 = mm_split(u1, inv_mid, NT) - mm_split(u0, inv_00, NT)
    v01 = -mm_split(u1, inv_01, NT)
    back(0, v00, v01)
    out[1] = landed(1)
    total = []
    for b in (0, 1):
        whole(r0.at[1:n, b], br.at[b])
        own = y0[b, rows_at(z, share), :]
        for k in range(1, n):
            own = own + r0[k, b]
        total.append(own)
    last = landed(0)
    for b in (0, 1):
        out[0, b] = last[b] + total[b]
    whole(pk.at[:, :, 0:3], sent.at[0])
    whole(cm.at[:, 0 : n - 1], sent.at[7])

    def finish(low):
        size = (7 + low // 2) * piece
        whole(tm.at[:, low:6, 0 : n - 1, 0:piece], sent.at[1])
        whole(tm.at[:, :, 0, 0:size], sent.at[5])
        whole(tm.at[:, 0:4, 0:2, 0:size], sent.at[6])

    by(z, finish)
    whole(r1.at[1:n], sent.at[2])
    whole(r0.at[1:n], sent.at[3])
    whole(orecv.at[:, 0 : n - 1], sent.at[4])


def fused(n, ancestor, panels, row_map, offsets, noise, inverse, inner_link, cross_link):
    share, block = inverse.shape[2:]
    lanes = ancestor.shape[1]
    w = lanes // n
    cols, rows = panels.shape[3], panels.shape[2]
    dma = pltpu.SemaphoreType.DMA
    hbm = pl.BlockSpec(memory_space=pltpu.HBM)
    args = (
        row_map, offsets, ancestor, jnp.swapaxes(panels, 2, 3), noise,
        inverse.reshape(4, share, block), inner_link, cross_link.reshape(4, share, block),
    )
    return pl.pallas_call(
        functools.partial(kernel, n),
        name="substitute",
        out_shape=jax.ShapeDtypeStruct((2, 2, share, lanes), F32),
        in_specs=[hbm] * 8,
        out_specs=pl.BlockSpec(memory_space=pltpu.VMEM),
        scratch_shapes=[
            pltpu.SMEM(row_map.shape, jnp.int32),
            pltpu.SMEM(offsets.shape, jnp.int32),
            pltpu.VMEM(ancestor.shape, F32),
            pltpu.VMEM(noise.shape, F32),
            pltpu.VMEM((2, 6, n, share, block // 2), F32),
            pltpu.VMEM((4, n, share, block), F32),
            pltpu.VMEM((2, 2, 4, cols, rows), F32),
            pltpu.VMEM((2, rows, lanes), F32),
            pltpu.VMEM((lanes, 2 * block), F32),
            pltpu.VMEM((2, lanes, block), F32),
            pltpu.VMEM((2, block, lanes), F32),
            pltpu.VMEM((n, 2, w, block), F32),
            pltpu.VMEM((n, 2, share, lanes), F32),
            pltpu.VMEM((2, n, w, 2 * share), F32),
            pltpu.VMEM((2, n, w, 2 * share), F32),
            dma((8,)), dma((8,)),
            dma((2, 2)), dma((2,)), dma((2, 2)),
            dma((3, n - 1)), dma((3, n - 1)), dma((3,)),
            dma((2,)), dma((2,)), dma((2,)),
        ],
        compiler_params=pltpu.CompilerParams(
            collective_id=0, has_side_effects=True, vmem_limit_bytes=40 * 1024 * 1024
        ),
    )(*[pltpu.with_memory_space_constraint(a, pltpu.HBM) for a in args])


def solution(mesh):
    placed = (
        P(("groups", "rows"), "samples"),
        P(None, None, "rows", "samples"),
        P(None, "rows"),
        P(),
        P("groups", "samples"),
        P(None, None, "rows", None),
        P(None, "rows", None),
        P(None, None, "rows", None),
    )
    n = mesh.shape["rows"]

    def local(ancestor, panels, row_map, offsets, noise, inverse, inner_link, cross_link):
        args = (ancestor, panels, row_map, offsets, noise, inverse, inner_link, cross_link)
        fits = (
            mesh.shape["groups"] == 2
            and mesh.shape["samples"] == 4
            and n == 4
            and ancestor.shape[1] == 128
            and inverse.shape[2] % 64 == 0
            and inverse.shape[3] == n * inverse.shape[2]
            and row_map.shape[1] % 128 == 0
        )
        return fused(n, *args) if fits else plain(*args)

    return jax.shard_map(
        local,
        mesh=mesh,
        in_specs=placed,
        out_specs=P(None, None, "rows", ("groups", "samples")),
        check_vma=False,
    )
```

```python
import functools

import jax
import jax.numpy as jnp
from jax import lax
from jax.experimental import pallas as pl
from jax.experimental.pallas import tpu as pltpu
from jax.sharding import PartitionSpec as P

F32 = jnp.float32
BF16 = jnp.bfloat16
NN = ((1,), (0,))
NT = ((1,), (1,))


def product(left, right):
    return jnp.dot(left, right, precision=lax.Precision.HIGHEST, preferred_element_type=F32)


def apply_inverse(target, partial_value, inverse_rows):
    rows_here = inverse_rows.shape[0]
    share = lax.psum_scatter(partial_value, "rows", scatter_dimension=0, tiled=True)
    first_own = lax.axis_index("rows") * rows_here
    residue = lax.dynamic_slice_in_dim(target, first_own, rows_here, 0) - share
    return product(inverse_rows, lax.all_gather(residue, "rows", axis=0, tiled=True))


def plain(ancestor, panels, row_map, offsets, noise, inverse, inner_link, cross_link):
    block_rows = inverse.shape[3]
    solved = [[None, None], [None, None]]
    for p in (1, 0):
        front_rows = jnp.take(ancestor, row_map[p], axis=0)
        window = lax.dynamic_slice_in_dim(noise, offsets[p], 2 * block_rows, 0)
        for b in (1, 0):
            whole = lax.all_gather(panels[p, b], "samples", axis=1, tiled=True)
            partial_value = product(whole.T, front_rows)
            if b == 0:
                partial_value = partial_value + product(inner_link[p].T, solved[p][1])
            if p == 0:
                for e in (0, 1):
                    partial_value = partial_value + product(cross_link[b, e].T, solved[1][e])
            target = window[b * block_rows : (b + 1) * block_rows]
            solved[p][b] = apply_inverse(target, partial_value, inverse[p, b])
    return jnp.stack([jnp.stack(solved[0]), jnp.stack(solved[1])])


def split(a):
    hi = a.astype(BF16)
    return hi, (a - hi.astype(F32)).astype(BF16)


def dot(a, b, dims):
    return lax.dot_general(a, b, (dims, ((), ())), preferred_element_type=F32)


def mm(a, b, dims):
    ah, al = split(a)
    bh, bl = split(b)
    m = a.shape[0]
    both = dot(jnp.concatenate([ah, al], 0), bh, dims)
    return both[:m] + (both[m:] + dot(ah, bl, dims))


def mm_split(a, pair, dims):
    ah, al = split(a)
    bh, bl = pair
    m = a.shape[0]
    both = dot(jnp.concatenate([ah, al], 0), bh, dims)
    return both[:m] + (both[m:] + dot(ah, bl, dims))


def kernel(
    n, rm_h, off_h, anc_h, pan_h, noise_h, inv_h, lnk_h, crs_h, out,
    rm, off, anc, nz, tm, cm, pk, fr, tt, y1, y0, r1, r0, osend, orecv,
    loc, sent, pxr, pcr, prr, zr, mr, cr, ar, br, osr,
):
    y = lax.axis_index("groups")
    z = lax.axis_index("rows")
    s = lax.axis_index("samples")
    x, c = s // 2, s % 2
    sx = (s + 2) % 4
    sib = s + 1 - 2 * c
    to_x, to_y, to_c = {"samples": sx}, {"groups": 1 - y}, {"samples": sib}
    to_d = {"groups": 1 - y, "samples": sx}
    block = cm.shape[3]
    share = cm.shape[2]
    left, right = slice(0, block // 2), slice(block // 2, block)
    piece = share // 8
    lanes = anc.shape[1]
    w = lanes // n
    up = [j + (j >= z).astype(jnp.int32) for j in range(n - 1)]

    barrier = pltpu.get_barrier_semaphore()
    peers = [{"rows": (z + k) % n} for k in range(1, n)] + [to_d, to_x, to_y, to_c]
    for peer in peers:
        pl.semaphore_signal(barrier, inc=1, device_id=peer, device_id_type=pl.DeviceIdType.MESH)

    local = [
        pltpu.make_async_copy(rm_h, rm, loc.at[0]),
        pltpu.make_async_copy(anc_h, anc, loc.at[1]),
        pltpu.make_async_copy(pan_h, pk.at[:, :, s], loc.at[2]),
        pltpu.make_async_copy(off_h, off, loc.at[3]),
        pltpu.make_async_copy(crs_h, cm.at[:, z], loc.at[5]),
        pltpu.make_async_copy(noise_h, nz, loc.at[4]),
    ]
    for g in (0, 1):
        for ref, at, side in (
            (inv_h.at[2 * g : 2 * g + 2], 0, left), (inv_h.at[2 * g : 2 * g + 2], 2, right),
            (lnk_h.at[g : g + 1], 4, left), (lnk_h.at[g : g + 1], 5, right),
        ):
            size = 2 if at < 4 else 1
            local.append(pltpu.make_async_copy(ref.at[:, :, side], tm.at[g, at : at + size, z], loc.at[6]))
    for copy in local[:2]:
        copy.start()

    def remote(src, dst, ss, rs, where):
        return pltpu.make_async_remote_copy(
            src_ref=src, dst_ref=dst, send_sem=ss, recv_sem=rs,
            device_id=where, device_id_type=pl.DeviceIdType.MESH,
        )

    def go(src, dst, ss, rs, where):
        remote(src, dst, sent.at[ss], rs, where).start()

    def whole(ref, sem):
        pltpu.make_async_copy(ref, ref, sem).wait()

    def rows_at(index, size):
        return pl.ds(pl.multiple_of(index * size, size), size)

    q = c * 4 + x * 2 + y
    def by(index, make):
        pl.when(index < n // 2)(lambda: make(0))
        pl.when(index >= n // 2)(lambda: make(2))

    def send_z(g):
        own = rows_at(q, piece)

        def make(low):
            for k in range(1, n):
                where = {"rows": (z + k) % n}
                pair = inv_h.at[2 * g : 2 * g + 2, own]
                if low == 0:
                    go(pair.at[:, :, left], tm.at[g, 0:2, z, own], 1, zr.at[g, k - 1], where)
                go(pair.at[:, :, right], tm.at[g, 2:4, z, own], 1, zr.at[g, k - 1], where)
                one = lnk_h.at[g : g + 1, own]
                go(one.at[:, :, left], tm.at[g, 4:5, z, own], 1, zr.at[g, k - 1], where)
                go(one.at[:, :, right], tm.at[g, 5:6, z, own], 1, zr.at[g, k - 1], where)

        if g < 2:
            by(z, make)
        else:
            for k in range(1, n):
                go(crs_h.at[:, own], cm.at[:, z, own], 7, zr.at[g, k - 1], {"rows": (z + k) % n})

    def send_p(p):
        for b in (1, 0):
            go(pan_h.at[p, b], pk.at[p, b, s], 0, pxr.at[p, b], to_x)
        go(pan_h.at[p], pk.at[p, :, s], 0, pcr.at[p], to_c)

    def relay_p(p, b):
        whole(pk.at[p, b, sx], pxr.at[p, b])
        go(pk.at[p, b, sx], pk.at[p, b, sx], 0, prr.at[p, b], to_c)

    def sibling_p(p):
        whole(pk.at[p, :, sib], pcr.at[p])

    def relayed_p(p, b):
        whole(pk.at[p, b, sib], prr.at[p, b])

    def gather(p):
        def rows8(i, carry):
            for r in range(8):
                fr[p, pl.ds(i * 8 + r, 1), :] = anc[pl.ds(rm[p, i * 8 + r], 1), :]
            return carry

        lax.fori_loop(0, fr.shape[1] // 8, rows8, 0)

    def spread(g):
        for k in range(1, n):
            zz = (z + n - k) % n

            def make(low):
                ref = tm.at[g, low:6, zz, rows_at(q, piece)] if g < 2 else cm.at[:, zz, rows_at(q, piece)]
                whole(ref, zr.at[g, k - 1])
                for where in (to_y, to_d, to_x):
                    go(ref, ref, 5 if g < 2 else 7, mr.at[g, k - 1], where)

            by(zz, make) if g < 2 else make(0)

    def join(g):
        for k in range(1, n):
            zz = (z + n - k) % n

            def make(low):
                whole(tm.at[g, low:6, zz, 0 : 3 * piece] if g < 2 else cm.at[:, zz, 0 : 3 * piece], mr.at[g, k - 1])
                own = rows_at(c, 4 * piece)
                ref = tm.at[g, low:6, zz, own] if g < 2 else cm.at[:, zz, own]
                go(ref, ref, 6 if g < 2 else 7, cr.at[g], to_c)

            by(zz, make) if g < 2 else make(0)

    def joined(g):
        if g < 2:
            by(z, lambda low: whole(tm.at[g, 0:4, 0:2, 0 : (7 + low // 2) * piece], cr.at[g]))
        else:
            whole(cm.at[:, 0 : n - 1, 0 : 4 * piece], cr.at[g])

    def matrix(g, i):
        return jnp.concatenate(
            [tm[g, at].reshape(block, block // 2) for at in ((i, i + 2) if i < 2 else (4, 5))], axis=1
        )

    def sums_1(b, fh, fb):
        ph, low = split(pk[1, b].reshape(block, block))
        both = dot(fb, ph, NT)
        y1[b] = both[:lanes] + (both[lanes:] + dot(fh, low, NT))
        for zz in up:
            k = (zz + n - z) % n
            go(y1.at[b, rows_at(zz, w)], r1.at[k, b], 2, ar.at[b], {"rows": zz})

    def sums_0(b, value):
        y0[b] = value
        for zz in up:
            k = (zz + n - z) % n
            go(y0.at[b, rows_at(zz, share)], r0.at[k, b], 3, br.at[b], {"rows": zz})

    def residue(b):
        whole(r1.at[1:n, b], ar.at[b])
        total = y1[b, rows_at(z, w), :]
        for k in range(1, n):
            total = total + r1[k, b]
        return tt[rows_at(z, w), b * block : (b + 1) * block] - total

    def back(p, first, second):
        for i in range(n):
            cut = slice(i * share, (i + 1) * share)
            osend[p, i] = jnp.concatenate([first[:, cut], second[:, cut]], axis=1)
        orecv[p, z] = osend[p, z]
        for zz in up:
            go(osend.at[p, zz], orecv.at[p, z], 4, osr.at[p], {"rows": zz})

    def landed(p):
        whole(orecv.at[p, 0 : n - 1], osr.at[p])
        return orecv[p].reshape(lanes, 2 * share).T.reshape(2, share, lanes)

    pl.semaphore_wait(barrier, len(peers))
    send_p(1)
    send_z(0)
    local[2].start()
    send_p(0)
    send_z(1)
    send_z(2)
    for g in (0, 1):
        tm[g, 0:2, n // 2 : n] = jnp.zeros((2, n - n // 2, share, block // 2), F32)
    for copy in local[3:]:
        copy.start()

    relay_p(1, 1)
    local[0].wait()
    local[1].wait()
    gather(1)
    fh, low = split(fr[1].T)
    fb = jnp.concatenate([fh, low], 0)
    relay_p(1, 0)
    spread(0)
    local[2].wait()
    sibling_p(1)
    relayed_p(1, 1)
    sums_1(1, fh, fb)
    relayed_p(1, 0)
    sums_1(0, fh, fb)
    gather(0)
    relay_p(0, 1)
    relay_p(0, 0)
    spread(1)
    local[3].wait()
    whole(cm.at[:, z], loc.at[5])
    whole(tm.at[:, :, z], loc.at[6])
    local[5].wait()
    sibling_p(0)
    rest = {}
    for b in (1, 0):
        relayed_p(0, b)
        rest[b] = nz[pl.ds(off[0] + b * block, block), :] * (1.0 / n) - mm(pk[0, b].reshape(block, block), fr[0], NN)
    spread(2)
    join(0)
    joined(0)
    part = mm(matrix(0, 1), rest[1], NN)
    sums_0(1, part)
    sums_0(0, mm(matrix(0, 0), rest[0] - mm(matrix(0, 2).T, part, NN), NN))
    joined_inverse = mm(matrix(0, 0), mm(matrix(0, 2).T, matrix(0, 1), NN), NN)
    inv_00, inv_01, inv_mid = split(matrix(0, 0)), split(matrix(0, 1)), split(joined_inverse)
    tt[...] = nz[pl.ds(off[1], 2 * block), :].T
    join(1)
    joined(1)
    s11 = mm(residue(1), matrix(1, 1), NT)
    s10 = mm(residue(0) - mm(s11, matrix(1, 2), NN), matrix(1, 0), NT)
    back(1, s10, s11)
    join(2)
    joined(2)
    s1 = jnp.concatenate([s10, s11], axis=1)
    u0 = mm(s1, cm[0:2].reshape(2 * block, block), NN)
    u1 = mm(s1, cm[2:4].reshape(2 * block, block), NN)
    v00 = mm_split(u1, inv_mid, NT) - mm_split(u0, inv_00, NT)
    v01 = -mm_split(u1, inv_01, NT)
    back(0, v00, v01)
    out[1] = landed(1)
    total = []
    for b in (0, 1):
        whole(r0.at[1:n, b], br.at[b])
        own = y0[b, rows_at(z, share), :]
        for k in range(1, n):
            own = own + r0[k, b]
        total.append(own)
    last = landed(0)
    for b in (0, 1):
        out[0, b] = last[b] + total[b]
    whole(pk.at[:, :, 0:3], sent.at[0])
    whole(cm.at[:, 0 : n - 1], sent.at[7])

    def finish(low):
        size = (7 + low // 2) * piece
        whole(tm.at[:, low:6, 0 : n - 1, 0:piece], sent.at[1])
        whole(tm.at[:, :, 0, 0:size], sent.at[5])
        whole(tm.at[:, 0:4, 0:2, 0:size], sent.at[6])

    by(z, finish)
    whole(r1.at[1:n], sent.at[2])
    whole(r0.at[1:n], sent.at[3])
    whole(orecv.at[:, 0 : n - 1], sent.at[4])


def fused(n, ancestor, panels, row_map, offsets, noise, inverse, inner_link, cross_link):
    share, block = inverse.shape[2:]
    lanes = ancestor.shape[1]
    w = lanes // n
    cols, rows = panels.shape[3], panels.shape[2]
    dma = pltpu.SemaphoreType.DMA
    hbm = pl.BlockSpec(memory_space=pltpu.HBM)
    args = (
        row_map, offsets, ancestor, jnp.swapaxes(panels, 2, 3), noise,
        inverse.reshape(4, share, block), inner_link, cross_link.reshape(4, share, block),
    )
    return pl.pallas_call(
        functools.partial(kernel, n),
        name="substitute",
        out_shape=jax.ShapeDtypeStruct((2, 2, share, lanes), F32),
        in_specs=[hbm] * 8,
        out_specs=pl.BlockSpec(memory_space=pltpu.VMEM),
        scratch_shapes=[
            pltpu.SMEM(row_map.shape, jnp.int32),
            pltpu.SMEM(offsets.shape, jnp.int32),
            pltpu.VMEM(ancestor.shape, F32),
            pltpu.VMEM(noise.shape, F32),
            pltpu.VMEM((2, 6, n, share, block // 2), F32),
            pltpu.VMEM((4, n, share, block), F32),
            pltpu.VMEM((2, 2, 4, cols, rows), F32),
            pltpu.VMEM((2, rows, lanes), F32),
            pltpu.VMEM((lanes, 2 * block), F32),
            pltpu.VMEM((2, lanes, block), F32),
            pltpu.VMEM((2, block, lanes), F32),
            pltpu.VMEM((n, 2, w, block), F32),
            pltpu.VMEM((n, 2, share, lanes), F32),
            pltpu.VMEM((2, n, w, 2 * share), F32),
            pltpu.VMEM((2, n, w, 2 * share), F32),
            dma((7,)), dma((8,)),
            dma((2, 2)), dma((2,)), dma((2, 2)),
            dma((3, n - 1)), dma((3, n - 1)), dma((3,)),
            dma((2,)), dma((2,)), dma((2,)),
        ],
        compiler_params=pltpu.CompilerParams(
            collective_id=0, has_side_effects=True, vmem_limit_bytes=40 * 1024 * 1024
        ),
    )(*[pltpu.with_memory_space_constraint(a, pltpu.HBM) for a in args])


def solution(mesh):
    placed = (
        P(("groups", "rows"), "samples"),
        P(None, None, "rows", "samples"),
        P(None, "rows"),
        P(),
        P("groups", "samples"),
        P(None, None, "rows", None),
        P(None, "rows", None),
        P(None, None, "rows", None),
    )
    n = mesh.shape["rows"]

    def local(ancestor, panels, row_map, offsets, noise, inverse, inner_link, cross_link):
        args = (ancestor, panels, row_map, offsets, noise, inverse, inner_link, cross_link)
        fits = (
            mesh.shape["groups"] == 2
            and mesh.shape["samples"] == 4
            and n == 4
            and ancestor.shape[1] == 128
            and inverse.shape[2] % 64 == 0
            and inverse.shape[3] == n * inverse.shape[2]
            and row_map.shape[1] % 128 == 0
        )
        return fused(n, *args) if fits else plain(*args)

    return jax.shard_map(
        local,
        mesh=mesh,
        in_specs=placed,
        out_specs=P(None, None, "rows", ("groups", "samples")),
        check_vma=False,
    )
```

```python
import functools

import jax
import jax.numpy as jnp
from jax import lax
from jax.experimental import pallas as pl
from jax.experimental.pallas import tpu as pltpu
from jax.sharding import PartitionSpec as P

F32 = jnp.float32
BF16 = jnp.bfloat16
NN = ((1,), (0,))
NT = ((1,), (1,))


def product(left, right):
    return jnp.dot(left, right, precision=lax.Precision.HIGHEST, preferred_element_type=F32)


def apply_inverse(target, partial_value, inverse_rows):
    rows_here = inverse_rows.shape[0]
    share = lax.psum_scatter(partial_value, "rows", scatter_dimension=0, tiled=True)
    first_own = lax.axis_index("rows") * rows_here
    residue = lax.dynamic_slice_in_dim(target, first_own, rows_here, 0) - share
    return product(inverse_rows, lax.all_gather(residue, "rows", axis=0, tiled=True))


def plain(ancestor, panels, row_map, offsets, noise, inverse, inner_link, cross_link):
    block_rows = inverse.shape[3]
    solved = [[None, None], [None, None]]
    for p in (1, 0):
        front_rows = jnp.take(ancestor, row_map[p], axis=0)
        window = lax.dynamic_slice_in_dim(noise, offsets[p], 2 * block_rows, 0)
        for b in (1, 0):
            whole = lax.all_gather(panels[p, b], "samples", axis=1, tiled=True)
            partial_value = product(whole.T, front_rows)
            if b == 0:
                partial_value = partial_value + product(inner_link[p].T, solved[p][1])
            if p == 0:
                for e in (0, 1):
                    partial_value = partial_value + product(cross_link[b, e].T, solved[1][e])
            target = window[b * block_rows : (b + 1) * block_rows]
            solved[p][b] = apply_inverse(target, partial_value, inverse[p, b])
    return jnp.stack([jnp.stack(solved[0]), jnp.stack(solved[1])])


def split(a):
    hi = a.astype(BF16)
    return hi, (a - hi.astype(F32)).astype(BF16)


def dot(a, b, dims):
    return lax.dot_general(a, b, (dims, ((), ())), preferred_element_type=F32)


def mm(a, b, dims):
    ah, al = split(a)
    bh, bl = split(b)
    m = a.shape[0]
    both = dot(jnp.concatenate([ah, al], 0), bh, dims)
    return both[:m] + (both[m:] + dot(ah, bl, dims))


def mm_split(a, pair, dims):
    ah, al = split(a)
    bh, bl = pair
    m = a.shape[0]
    both = dot(jnp.concatenate([ah, al], 0), bh, dims)
    return both[:m] + (both[m:] + dot(ah, bl, dims))


def kernel(
    n, rm_h, off_h, anc_h, pan_h, noise_h, inv_h, lnk_h, crs_h, out,
    rm, off, anc, nz, tm, cm, pk, fr, tt, y1, y0, r1, r0, osend, orecv,
    loc, sent, pxr, pcr, prr, zr, mr, cr, ar, br, osr,
):
    y = lax.axis_index("groups")
    z = lax.axis_index("rows")
    s = lax.axis_index("samples")
    x, c = s // 2, s % 2
    sx = (s + 2) % 4
    sib = s + 1 - 2 * c
    to_x, to_y, to_c = {"samples": sx}, {"groups": 1 - y}, {"samples": sib}
    to_d = {"groups": 1 - y, "samples": sx}
    block = cm.shape[3]
    share = cm.shape[2]
    left, right = slice(0, block // 2), slice(block // 2, block)
    piece = share // 8
    lanes = anc.shape[1]
    w = lanes // n
    up = [j + (j >= z).astype(jnp.int32) for j in range(n - 1)]

    barrier = pltpu.get_barrier_semaphore()
    peers = [{"rows": (z + k) % n} for k in range(1, n)] + [to_d, to_x, to_y, to_c]
    for peer in peers:
        pl.semaphore_signal(barrier, inc=1, device_id=peer, device_id_type=pl.DeviceIdType.MESH)

    local = [
        pltpu.make_async_copy(rm_h, rm, loc.at[0]),
        pltpu.make_async_copy(anc_h, anc, loc.at[1]),
        pltpu.make_async_copy(pan_h, pk.at[:, :, s], loc.at[2]),
        pltpu.make_async_copy(off_h, off, loc.at[3]),
        pltpu.make_async_copy(crs_h, cm.at[:, z], loc.at[5]),
        pltpu.make_async_copy(noise_h, nz, loc.at[4]),
    ]
    for g in (0, 1):
        for ref, at, side in (
            (inv_h.at[2 * g : 2 * g + 2], 0, left), (inv_h.at[2 * g : 2 * g + 2], 2, right),
            (lnk_h.at[g : g + 1], 4, left), (lnk_h.at[g : g + 1], 5, right),
        ):
            size = 2 if at < 4 else 1
            local.append(pltpu.make_async_copy(ref.at[:, :, side], tm.at[g, at : at + size, z], loc.at[6]))
    for copy in local[:2]:
        copy.start()

    def remote(src, dst, ss, rs, where):
        return pltpu.make_async_remote_copy(
            src_ref=src, dst_ref=dst, send_sem=ss, recv_sem=rs,
            device_id=where, device_id_type=pl.DeviceIdType.MESH,
        )

    def go(src, dst, ss, rs, where):
        remote(src, dst, sent.at[ss], rs, where).start()

    def whole(ref, sem):
        pltpu.make_async_copy(ref, ref, sem).wait()

    def rows_at(index, size):
        return pl.ds(pl.multiple_of(index * size, size), size)

    q = c * 4 + x * 2 + y
    def by(index, make):
        pl.when(index < n // 2)(lambda: make(0))
        pl.when(index >= n // 2)(lambda: make(2))

    def send_z(g):
        own = rows_at(q, piece)

        def make(low):
            for k in range(1, n):
                where = {"rows": (z + k) % n}
                pair = inv_h.at[2 * g : 2 * g + 2, own]
                if low == 0:
                    go(pair.at[:, :, left], tm.at[g, 0:2, z, own], 1, zr.at[g, k - 1], where)
                go(pair.at[:, :, right], tm.at[g, 2:4, z, own], 1, zr.at[g, k - 1], where)
                one = lnk_h.at[g : g + 1, own]
                go(one.at[:, :, left], tm.at[g, 4:5, z, own], 1, zr.at[g, k - 1], where)
                go(one.at[:, :, right], tm.at[g, 5:6, z, own], 1, zr.at[g, k - 1], where)

        if g < 2:
            by(z, make)
        else:
            for k in range(1, n):
                go(crs_h.at[:, own], cm.at[:, z, own], 7, zr.at[g, k - 1], {"rows": (z + k) % n})

    def send_p(p):
        for b in (1, 0):
            go(pan_h.at[p, b], pk.at[p, b, s], 0, pxr.at[p, b], to_x)
        go(pan_h.at[p], pk.at[p, :, s], 0, pcr.at[p], to_c)

    def relay_p(p, b):
        whole(pk.at[p, b, sx], pxr.at[p, b])
        go(pk.at[p, b, sx], pk.at[p, b, sx], 0, prr.at[p, b], to_c)

    def sibling_p(p):
        whole(pk.at[p, :, sib], pcr.at[p])

    def relayed_p(p, b):
        whole(pk.at[p, b, sib], prr.at[p, b])

    def gather(p):
        def rows8(i, carry):
            for r in range(8):
                fr[p, pl.ds(i * 8 + r, 1), :] = anc[pl.ds(rm[p, i * 8 + r], 1), :]
            return carry

        lax.fori_loop(0, fr.shape[1] // 8, rows8, 0)

    def spread(g):
        for k in range(1, n):
            zz = (z + n - k) % n

            def make(low):
                ref = tm.at[g, low:6, zz, rows_at(q, piece)] if g < 2 else cm.at[:, zz, rows_at(q, piece)]
                whole(ref, zr.at[g, k - 1])
                for where in (to_y, to_d, to_x):
                    go(ref, ref, 5 if g < 2 else 7, mr.at[g, k - 1], where)

            by(zz, make) if g < 2 else make(0)

    def join(g):
        for k in range(1, n):
            zz = (z + n - k) % n

            def make(low):
                whole(tm.at[g, low:6, zz, 0 : 3 * piece] if g < 2 else cm.at[:, zz, 0 : 3 * piece], mr.at[g, k - 1])
                own = rows_at(c, 4 * piece)
                ref = tm.at[g, low:6, zz, own] if g < 2 else cm.at[:, zz, own]
                go(ref, ref, 6 if g < 2 else 7, cr.at[g], to_c)

            by(zz, make) if g < 2 else make(0)

    def joined(g):
        if g < 2:
            by(z, lambda low: whole(tm.at[g, 0:4, 0:2, 0 : (7 + low // 2) * piece], cr.at[g]))
        else:
            whole(cm.at[:, 0 : n - 1, 0 : 4 * piece], cr.at[g])

    def matrix(g, i):
        return jnp.concatenate(
            [tm[g, at].reshape(block, block // 2) for at in ((i, i + 2) if i < 2 else (4, 5))], axis=1
        )

    def sums_1(b, fh, fb):
        ph, low = split(pk[1, b].reshape(block, block))
        both = dot(fb, ph, NT)
        y1[b] = both[:lanes] + (both[lanes:] + dot(fh, low, NT))
        for zz in up:
            k = (zz + n - z) % n
            go(y1.at[b, rows_at(zz, w)], r1.at[k, b], 2, ar.at[b], {"rows": zz})

    def sums_0(b, value):
        y0[b] = value
        for zz in up:
            k = (zz + n - z) % n
            go(y0.at[b, rows_at(zz, share)], r0.at[k, b], 3, br.at[b], {"rows": zz})

    def residue(b):
        whole(r1.at[1:n, b], ar.at[b])
        total = y1[b, rows_at(z, w), :]
        for k in range(1, n):
            total = total + r1[k, b]
        return tt[rows_at(z, w), b * block : (b + 1) * block] - total

    def back(p, first, second):
        for i in range(n):
            cut = slice(i * share, (i + 1) * share)
            osend[p, i] = jnp.concatenate([first[:, cut], second[:, cut]], axis=1)
        orecv[p, z] = osend[p, z]
        for zz in up:
            go(osend.at[p, zz], orecv.at[p, z], 4, osr.at[p], {"rows": zz})

    def landed(p):
        whole(orecv.at[p, 0 : n - 1], osr.at[p])
        return orecv[p].reshape(lanes, 2 * share).T.reshape(2, share, lanes)

    pl.semaphore_wait(barrier, len(peers))
    send_p(1)
    send_z(0)
    local[2].start()
    send_p(0)
    send_z(1)
    send_z(2)
    for g in (0, 1):
        tm[g, 0:2, n // 2 : n] = jnp.zeros((2, n - n // 2, share, block // 2), F32)
    for copy in local[3:]:
        copy.start()

    local[0].wait()
    local[1].wait()
    gather(1)
    fh, low = split(fr[1].T)
    fb = jnp.concatenate([fh, low], 0)
    relay_p(1, 1)
    relay_p(1, 0)
    spread(0)
    local[2].wait()
    sibling_p(1)
    relayed_p(1, 1)
    sums_1(1, fh, fb)
    relayed_p(1, 0)
    sums_1(0, fh, fb)
    gather(0)
    relay_p(0, 1)
    relay_p(0, 0)
    spread(1)
    local[3].wait()
    whole(cm.at[:, z], loc.at[5])
    whole(tm.at[:, :, z], loc.at[6])
    local[5].wait()
    sibling_p(0)
    rest = {}
    for b in (1, 0):
        relayed_p(0, b)
        rest[b] = nz[pl.ds(off[0] + b * block, block), :] * (1.0 / n) - mm(pk[0, b].reshape(block, block), fr[0], NN)
    spread(2)
    tt[...] = nz[pl.ds(off[1], 2 * block), :].T
    join(0)
    joined(0)
    part = mm(matrix(0, 1), rest[1], NN)
    sums_0(1, part)
    sums_0(0, mm(matrix(0, 0), rest[0] - mm(matrix(0, 2).T, part, NN), NN))
    joined_inverse = mm(matrix(0, 0), mm(matrix(0, 2).T, matrix(0, 1), NN), NN)
    inv_00, inv_01, inv_mid = split(matrix(0, 0)), split(matrix(0, 1)), split(joined_inverse)
    join(1)
    joined(1)
    low_11, low_10, link_1 = split(matrix(1, 1)), split(matrix(1, 0)), split(matrix(1, 2))
    s11 = mm_split(residue(1), low_11, NT)
    s10 = mm_split(residue(0) - mm_split(s11, link_1, NN), low_10, NT)
    back(1, s10, s11)
    join(2)
    joined(2)
    s1 = jnp.concatenate([s10, s11], axis=1)
    u0 = mm(s1, cm[0:2].reshape(2 * block, block), NN)
    u1 = mm(s1, cm[2:4].reshape(2 * block, block), NN)
    v00 = mm_split(u1, inv_mid, NT) - mm_split(u0, inv_00, NT)
    v01 = -mm_split(u1, inv_01, NT)
    back(0, v00, v01)
    out[1] = landed(1)
    total = []
    for b in (0, 1):
        whole(r0.at[1:n, b], br.at[b])
        own = y0[b, rows_at(z, share), :]
        for k in range(1, n):
            own = own + r0[k, b]
        total.append(own)
    last = landed(0)
    for b in (0, 1):
        out[0, b] = last[b] + total[b]
    whole(pk.at[:, :, 0:3], sent.at[0])
    whole(cm.at[:, 0 : n - 1], sent.at[7])

    def finish(low):
        size = (7 + low // 2) * piece
        whole(tm.at[:, low:6, 0 : n - 1, 0:piece], sent.at[1])
        whole(tm.at[:, :, 0, 0:size], sent.at[5])
        whole(tm.at[:, 0:4, 0:2, 0:size], sent.at[6])

    by(z, finish)
    whole(r1.at[1:n], sent.at[2])
    whole(r0.at[1:n], sent.at[3])
    whole(orecv.at[:, 0 : n - 1], sent.at[4])


def fused(n, ancestor, panels, row_map, offsets, noise, inverse, inner_link, cross_link):
    share, block = inverse.shape[2:]
    lanes = ancestor.shape[1]
    w = lanes // n
    cols, rows = panels.shape[3], panels.shape[2]
    dma = pltpu.SemaphoreType.DMA
    hbm = pl.BlockSpec(memory_space=pltpu.HBM)
    args = (
        row_map, offsets, ancestor, jnp.swapaxes(panels, 2, 3), noise,
        inverse.reshape(4, share, block), inner_link, cross_link.reshape(4, share, block),
    )
    return pl.pallas_call(
        functools.partial(kernel, n),
        name="substitute",
        out_shape=jax.ShapeDtypeStruct((2, 2, share, lanes), F32),
        in_specs=[hbm] * 8,
        out_specs=pl.BlockSpec(memory_space=pltpu.VMEM),
        scratch_shapes=[
            pltpu.SMEM(row_map.shape, jnp.int32),
            pltpu.SMEM(offsets.shape, jnp.int32),
            pltpu.VMEM(ancestor.shape, F32),
            pltpu.VMEM(noise.shape, F32),
            pltpu.VMEM((2, 6, n, share, block // 2), F32),
            pltpu.VMEM((4, n, share, block), F32),
            pltpu.VMEM((2, 2, 4, cols, rows), F32),
            pltpu.VMEM((2, rows, lanes), F32),
            pltpu.VMEM((lanes, 2 * block), F32),
            pltpu.VMEM((2, lanes, block), F32),
            pltpu.VMEM((2, block, lanes), F32),
            pltpu.VMEM((n, 2, w, block), F32),
            pltpu.VMEM((n, 2, share, lanes), F32),
            pltpu.VMEM((2, n, w, 2 * share), F32),
            pltpu.VMEM((2, n, w, 2 * share), F32),
            dma((7,)), dma((8,)),
            dma((2, 2)), dma((2,)), dma((2, 2)),
            dma((3, n - 1)), dma((3, n - 1)), dma((3,)),
            dma((2,)), dma((2,)), dma((2,)),
        ],
        compiler_params=pltpu.CompilerParams(
            collective_id=0, has_side_effects=True, vmem_limit_bytes=40 * 1024 * 1024
        ),
    )(*[pltpu.with_memory_space_constraint(a, pltpu.HBM) for a in args])


def solution(mesh):
    placed = (
        P(("groups", "rows"), "samples"),
        P(None, None, "rows", "samples"),
        P(None, "rows"),
        P(),
        P("groups", "samples"),
        P(None, None, "rows", None),
        P(None, "rows", None),
        P(None, None, "rows", None),
    )
    n = mesh.shape["rows"]

    def local(ancestor, panels, row_map, offsets, noise, inverse, inner_link, cross_link):
        args = (ancestor, panels, row_map, offsets, noise, inverse, inner_link, cross_link)
        fits = (
            mesh.shape["groups"] == 2
            and mesh.shape["samples"] == 4
            and n == 4
            and ancestor.shape[1] == 128
            and inverse.shape[2] % 64 == 0
            and inverse.shape[3] == n * inverse.shape[2]
            and row_map.shape[1] % 128 == 0
        )
        return fused(n, *args) if fits else plain(*args)

    return jax.shard_map(
        local,
        mesh=mesh,
        in_specs=placed,
        out_specs=P(None, None, "rows", ("groups", "samples")),
        check_vma=False,
    )
```
